32 devices in a mesh: groups: 2 (over x), blk: 16 (over z, y, core).
Axes of the slice: x: 2, y: 2, z: 4, core: 2. Of those that a mesh axis runs over, the one named last changes fastest.
Arguments:
- query_inputs: bfloat16 [8192, 4096], P(('groups', 'blk')), parts along dimension 0, may hold values from -6 to 6
- query_grads: bfloat16 [8192, 4096], P(('groups', 'blk')), parts along dimension 0, may hold values from -6 to 6
- proj_in: bfloat16 [4096, 64], replicated, may hold values from -0.09375 to 0.09375
- proj_out: bfloat16 [4096, 64], replicated, may hold values from -0.09375 to 0.09375
- train_rows: bfloat16 [8192, 4096], P(('groups', 'blk')), parts along dimension 0, may hold values from -0.09375 to 0.09375
- token_owner: int32 [8192, 1], P(('groups', 'blk')), parts along dimension 0, may hold values from 0 to 15; in each aligned block of 256 rows (0 to 255, 256 to 511, ...) at most 64 rows name the same one
- token_slot: int32 [8192], P(('groups', 'blk')), parts along dimension 0, may hold values from 0 to 31
Outputs:
- influence: bfloat16 [12, 32, 8192], P(None, None, ('groups', 'blk')), parts along dimension 2
The draws below stay inside these ranges and needn't reach their ends.
There are 2 independent parts, one for each index of `groups`. The reference program is written for one: setup_inputs(seed, part) draws one part's arguments, and reference() takes and returns one part's arrays. A program takes and returns all parts, laid end to end along the dimension named above; an argument that names none is the same for every part. Nothing has to cross between parts.
Inputs may be any that keep to these rules, and one draw needn't show every extreme that they name: `token_owner`: within the tokens of one device no owner is named by more than 64 tokens, a bound that some block reaches.
All inputs are finite; a program needn't handle non-finite values. Where the reference program divides by a largest or mean magnitude, that divisor is 1e-20 or more.
Results may differ from the reference program's by a relative error of at most 0.0069.
Values may be sent and summed in bfloat16 or wider, within the bound.
A program may use at most 64 MiB of HBM per device.

```python
import math
import jax
import jax.numpy as jnp
import numpy as np
from jax import lax

D = 4096
R = 64
TOK_DEV = 256
DOC_DEV = 32
TR_DEV = 256
STOPS = 12
NEWTON_STEPS = 6
LEAD = 5
OWNERS = 16
CAP = 64
TOKENS = 4096
TRAIN = 4096


def place_ends(array, stream_key, least, high):
    spot = [jax.random.randint(jax.random.fold_in(stream_key, axis), (), 0, length) for axis, length in enumerate(array.shape)]
    main_axis = array.shape.index(max(array.shape))
    beside = spot[:main_axis] + [(spot[main_axis] + 1) % array.shape[main_axis]] + spot[main_axis + 1:]
    return array.at[tuple(spot)].set(least).at[tuple(beside)].set(high)


def level_of(key, dims, cuts, low, top_value):
    def one(position, blocks):
        draws = jax.random.uniform(jax.random.fold_in(jax.random.fold_in(key, 6), position), (blocks,), jnp.float32, low / len(cuts), top_value / len(cuts))
        return jnp.repeat(jnp.exp(draws), dims[position] // blocks).reshape((-1,) + (1,) * (len(dims) - position - 1))

    factor_of = one(*cuts[0])
    for cut in cuts[1:]:
        factor_of = factor_of * one(*cut)
    return factor_of


def deal_out(stream_key, own, number, rows, count, top, limit, skew):
    ranking = jax.random.permutation(stream_key, count)
    crowded, common = load_shares(count, rows * top, limit, skew, True), load_shares(count, rows * top, limit, skew, False)
    places = jnp.arange(count)

    def named(sizes, offset_by):
        used = int((sizes > 0).sum())
        fixed = max(1, used // 4)
        passed = fixed + (places - fixed + offset_by * (used - fixed)) % max(1, count - fixed)
        return jnp.zeros((count,), jnp.int32).at[ranking[jnp.where(places < fixed, places, passed)]].set(jnp.asarray(sizes, jnp.int32))

    sizes = jnp.where(number % 4 == 0, named(crowded, number // 4), named(common, number - number // 4 - 1))
    mixed = jax.random.permutation(jax.random.fold_in(own, 3), count)
    giver, receiver = mixed[0:count // 2 * 2:2], mixed[1:count // 2 * 2:2]
    slack = jnp.minimum(sizes[giver] - 1, limit - sizes[receiver]) // 2
    slack = jnp.where((giver == ranking[0]) | (receiver == ranking[0]) | (sizes[receiver] == 0), 0, jnp.maximum(slack, 0))
    passed = jax.random.randint(jax.random.fold_in(own, 4), (count // 2,), 0, 1 << 20) % (slack + 1)
    sizes = sizes.at[giver].add(-passed).at[receiver].add(passed)
    labels = jnp.searchsorted(jnp.cumsum(sizes), jnp.arange(rows * top), side="right").astype(jnp.int32)
    table = labels.reshape(top, rows).T
    table = table[jax.random.permutation(jax.random.fold_in(own, 1), rows)]
    offset_by = jax.random.randint(jax.random.fold_in(own, 2), (rows, 1), 0, top)
    return jnp.take_along_axis(table, (jnp.arange(top)[None, :] + offset_by) % top, axis=1)


def load_shares(amount, total, reach, lean, full):
    portions = [(1 << 20) // math.isqrt(standing ** lean) + 1 for standing in range(1, amount + 1)]
    largest = reach if full else min(reach, max(-(-total // amount), total * portions[0] // sum(portions)))
    least = 1 if total - largest >= amount - 1 else 0
    holding, spare = [largest] + [least] * (amount - 1), total - largest - least * (amount - 1)
    while spare > 0:
        candidates = [i for i in range(1, amount) if holding[i] < largest] or [i for i in range(1, amount) if holding[i] < reach]
        mass, left = sum([portions[i] for i in candidates]), spare
        for i in candidates:
            extra = min(reach - holding[i], max(1, left * portions[i] // mass), spare)
            holding[i] = holding[i] + extra
            spare = spare - extra
    return np.array(holding)


def bell_draw(key, extent, deviation, bound, cuts=(), held_as=jnp.bfloat16):
    drawn = deviation * jax.random.normal(key, extent, jnp.float32)
    if cuts:
        drawn = drawn * level_of(key, extent, cuts, -0.22, 0.18)
    return jnp.clip(drawn, -bound, bound).astype(held_as)


def setup_inputs(seed: int = 0, part: int = 0) -> dict:
    seeds = jax.random.split(jax.random.key(seed), 8)
    part_keys = jax.random.split(jax.random.fold_in(seeds[7], part), 8)
    query_inputs = bell_draw(part_keys[0], (TOKENS, D), 1.0, 6.0, ((0, 16),))
    query_grads = bell_draw(part_keys[1], (TOKENS, D), 1.0, 6.0, ((0, 16),))
    proj_in = bell_draw(seeds[2], (D, R), D ** -0.5, 0.09375)
    proj_out = bell_draw(seeds[3], (D, R), D ** -0.5, 0.09375)
    train_rows = bell_draw(part_keys[4], (TRAIN, R * R), (R * R) ** -0.5, 0.09375, ((0, 16),))
    token_owner_keys = jax.random.split(jax.random.fold_in(part_keys[5], 1), TOKENS // TOK_DEV)
    token_owner_turns = jax.random.permutation(jax.random.fold_in(part_keys[5], 3), TOKENS // TOK_DEV)
    token_owner = jax.vmap(lambda own, number: deal_out(jax.random.fold_in(part_keys[5], 2), own, number, TOK_DEV, OWNERS, 1, CAP, 2))(token_owner_keys, token_owner_turns).reshape((TOKENS, 1))
    token_slot = place_ends(jax.random.randint(part_keys[6], (TOKENS,), 0, DOC_DEV), jax.random.fold_in(part_keys[6], 1), 0, DOC_DEV - 1).astype(jnp.int32)
    return {"query_inputs": query_inputs, "query_grads": query_grads, "proj_in": proj_in, "proj_out": proj_out, "train_rows": train_rows, "token_owner": token_owner, "token_slot": token_slot}


HIGHEST_PRECISION = lax.Precision.HIGHEST


def inverse_factor(gram_sum, counts):
    width_low = gram_sum.shape[1]
    identity_mat = jnp.eye(width_low, dtype=jnp.float32)
    damped = gram_sum / (counts[:, None, None] + 1.0) + identity_mat[None]
    row_bound = jnp.max(jnp.sum(jnp.abs(damped), axis=2), axis=1)
    approx = identity_mat[None] / row_bound[:, None, None]
    for iteration in range(NEWTON_STEPS):
        product = jnp.einsum("dab,dbc->dac", damped, approx, precision=HIGHEST_PRECISION)
        approx = jnp.einsum("dab,dbc->dac", approx, 2.0 * identity_mat[None] - product, precision=HIGHEST_PRECISION)
    return approx


def reference(query_inputs, query_grads, proj_in, proj_out, train_rows, token_owner, token_slot):
    grads_low = jnp.dot(query_grads, proj_out, preferred_element_type=jnp.float32).astype(jnp.bfloat16)
    inputs_low = jnp.dot(query_inputs, proj_in, preferred_element_type=jnp.float32).astype(jnp.bfloat16)
    doc_ids = (token_owner[:, 0] * DOC_DEV + token_slot).astype(jnp.int32)
    doc_total = OWNERS * DOC_DEV

    def accumulate(carried, index):
        grad_sum, input_sum, count_sum = carried
        start = (index * TOK_DEV).astype(jnp.int32)
        grads_part = lax.dynamic_slice_in_dim(grads_low, start, TOK_DEV, 0).astype(jnp.float32)
        inputs_part = lax.dynamic_slice_in_dim(inputs_low, start, TOK_DEV, 0).astype(jnp.float32)
        ids_part = lax.dynamic_slice_in_dim(doc_ids, start, TOK_DEV, 0)
        joined = jnp.concatenate([grads_part, inputs_part], axis=1)
        grad_terms = grads_part[:, :, None] * joined[:, None, :]
        input_terms = inputs_part[:, :, None] * inputs_part[:, None, :]
        grad_sum = grad_sum.at[ids_part].add(grad_terms)
        input_sum = input_sum.at[ids_part].add(input_terms)
        count_sum = count_sum.at[ids_part].add(jnp.ones((TOK_DEV,), jnp.float32))
        return (grad_sum, input_sum, count_sum), None

    start_sums = (jnp.zeros((doc_total, R, 2 * R), jnp.float32), jnp.zeros((doc_total, R, R), jnp.float32), jnp.zeros((doc_total,), jnp.float32))
    sums_done, unused = lax.scan(accumulate, start_sums, jnp.arange(OWNERS, dtype=jnp.int32))
    grad_sum, input_sum, count_sum = sums_done
    outer_b = grad_sum[:, :, :R]
    doc_grad = grad_sum[:, :, R:]
    inv_a = inverse_factor(input_sum, count_sum)
    inv_b = inverse_factor(outer_b, count_sum)
    tilted = jnp.einsum("dab,dbc->dac", inv_b, doc_grad, precision=HIGHEST_PRECISION)
    tilted = jnp.einsum("dab,dbc->dac", tilted, inv_a, precision=HIGHEST_PRECISION)
    queries = tilted.reshape(OWNERS, DOC_DEV, R * R).astype(jnp.bfloat16)
    train_blocks = train_rows.reshape(OWNERS, TR_DEV, R * R)
    offsets = jnp.arange(STOPS, dtype=jnp.int32)

    def one_device(index):
        sources = (index - offsets + LEAD) % OWNERS
        visiting = queries[sources].astype(jnp.float32)
        resident = train_blocks[index].astype(jnp.float32)
        return jnp.einsum("skf,tf->skt", visiting, resident).astype(jnp.bfloat16)

    tile_rows = lax.map(one_device, jnp.arange(OWNERS, dtype=jnp.int32))
    return jnp.transpose(tile_rows, (1, 2, 0, 3)).reshape(STOPS, DOC_DEV, OWNERS * TR_DEV)
```

```python
import functools

import jax
import jax.numpy as jnp
from jax import lax
from jax.experimental import pallas as pl
from jax.experimental.pallas import tpu as pltpu
from jax.sharding import PartitionSpec as P

DOC_DEV = 32
STOPS = 12
NEWTON_STEPS = 6
LEAD = 5
LANES = 128
DOC_GROUP = 8
GROUPS = DOC_DEV // DOC_GROUP
MESH = pl.DeviceIdType.MESH
VMEM_SPEC = pl.BlockSpec(memory_space=pltpu.VMEM)
F32 = jnp.float32
BF16 = jnp.bfloat16
CONTRACT_LAST = (((1,), (1,)), ((), ()))


def matmul(left, right):
    return jnp.dot(left, right, preferred_element_type=F32)


def halves(value):
    high = value.astype(BF16)
    return high, (value - high.astype(F32)).astype(BF16)


def left_parts(value, right_half):
    width = value.shape[1] // 2
    high = value.astype(BF16).astype(F32)
    low = value - high
    if right_half:
        high = pltpu.roll(high, width, 1)
    else:
        low = pltpu.roll(low, width, 1)
    is_left = lax.broadcasted_iota(jnp.int32, value.shape, 1) < width
    parts = jnp.where(is_left, high, low).astype(BF16)
    return jnp.concatenate([parts, parts], axis=1)


def pair_product(lefts, rights, right_half):
    high, low = zip(*[halves(value) for value in rights])
    high, low = jnp.concatenate(high, axis=1), jnp.concatenate(low, axis=1)
    product = matmul(
        jnp.concatenate([left_parts(value, right_half) for value in lefts], axis=0),
        jnp.concatenate([high, high, low, low], axis=0),
    )
    rows, cols = lefts[0].shape
    return product[:rows, :cols], product[rows:, cols:]


def dispatch_kernel(owners, capacity, far_in, far_grad, p_in, p_out, owner_row, slot_row,
                    recv_rows, recv_slot, x_in, x_grad, fetched, low, send_rows, send_slot,
                    rows_sent, rows_here, slot_sent, slot_here):
    me = lax.axis_index("blk")
    fetch_grad = pltpu.make_async_copy(far_grad, x_grad, fetched.at[0])
    fetch_in = pltpu.make_async_copy(far_in, x_in, fetched.at[1])
    fetch_grad.start()
    fetch_in.start()
    barrier = pltpu.get_barrier_semaphore()

    @pl.loop(1, owners)
    def _(ahead):
        pl.semaphore_signal(
            barrier, inc=1, device_id={"blk": lax.rem(me + ahead, owners)}, device_id_type=MESH
        )

    count = x_in.shape[0]
    width = p_in.shape[0]
    token = lax.broadcasted_iota(jnp.int32, (count, count), 0)
    other = lax.broadcasted_iota(jnp.int32, (count, count), 1)
    earlier = jnp.where(token < other, 1.0, 0.0).astype(BF16)
    owner_id = lax.broadcasted_iota(jnp.int32, (owners, count), 0)
    owner_hot = jnp.where(owner_id == owner_row[...], 1.0, 0.0)
    before = matmul(owner_hot.astype(BF16), earlier)
    rank = jnp.sum(before * owner_hot, axis=0, keepdims=True).astype(jnp.int32)
    position = owner_row[...] * capacity + rank
    place = lax.broadcasted_iota(jnp.int32, (owners * capacity, count), 0)
    placed = jnp.where(place == position, 1.0, 0.0).astype(BF16)
    for at, values, weights, fetch in (
        (0, x_grad, p_out, fetch_grad), (width, x_in, p_in, fetch_in)
    ):
        fetch.wait()
        low[:, at:at + width] = lax.dot_general(
            values[...], weights[...], CONTRACT_LAST, preferred_element_type=F32
        ).astype(BF16)
    send_rows[...] = matmul(placed, low[...]).astype(BF16).reshape(send_rows.shape)
    coded = jnp.where(owner_id == owner_row[...], slot_row[...] + 1, 0).astype(F32).astype(BF16)
    lane = lax.broadcasted_iota(jnp.int32, (LANES, count), 0)
    shift = lax.rem(me, LANES // capacity) * capacity
    spread = jnp.where(lane == rank + shift, 1.0, 0.0).astype(BF16)
    codes = lax.dot_general(coded, spread, CONTRACT_LAST, preferred_element_type=F32)
    codes = codes.astype(jnp.int32)
    for owner in range(owners):
        send_slot[owner] = codes[owner:owner + 1]
    pl.semaphore_wait(barrier, owners - 1)

    def copies(target, source, sem):
        to = {"blk": target}
        return (
            pltpu.make_async_remote_copy(
                src_ref=send_rows.at[target], dst_ref=recv_rows.at[source],
                send_sem=rows_sent.at[target], recv_sem=rows_here.at[sem],
                device_id=to, device_id_type=MESH),
            pltpu.make_async_remote_copy(
                src_ref=send_slot.at[target], dst_ref=recv_slot.at[source],
                send_sem=slot_sent.at[target], recv_sem=slot_here.at[sem],
                device_id=to, device_id_type=MESH),
        )

    @pl.loop(1, owners)
    def _(ahead):
        for copy in copies(lax.rem(me + ahead, owners), me, me):
            copy.start()

    recv_rows[me] = send_rows[me]
    recv_slot[me] = send_slot[me]

    @pl.loop(1, owners)
    def _(ahead):
        source = lax.rem(me + ahead, owners)
        for copy in copies(source, source, source):
            copy.wait_recv()

    @pl.loop(1, owners)
    def _(ahead):
        for copy in copies(lax.rem(me + ahead, owners), me, me):
            copy.wait_send()


def dispatch(x_in, x_grad, p_in, p_out, owner_row, slot_row):
    owners = lax.axis_size("blk")
    count, width = x_in.shape[0], p_in.shape[0]
    capacity = 4 * count // owners
    rows = (owners, capacity, 2 * width)
    slots = (owners, 1, LANES)
    return pl.pallas_call(
        functools.partial(dispatch_kernel, owners, capacity),
        out_shape=(jax.ShapeDtypeStruct(rows, BF16), jax.ShapeDtypeStruct(slots, jnp.int32)),
        in_specs=[pl.BlockSpec(memory_space=pl.ANY)] * 2 + [VMEM_SPEC] * 4,
        out_specs=(VMEM_SPEC, VMEM_SPEC),
        scratch_shapes=[
            pltpu.VMEM(x_in.shape, BF16),
            pltpu.VMEM(x_in.shape, BF16),
            pltpu.SemaphoreType.DMA((2,)),
            pltpu.VMEM((count, 2 * width), BF16),
            pltpu.VMEM(rows, BF16),
            pltpu.VMEM(slots, jnp.int32),
        ] + [pltpu.SemaphoreType.DMA((owners,))] * 4,
        compiler_params=pltpu.CompilerParams(collective_id=0, has_side_effects=True),
        name="dispatch",
    )(x_in, x_grad, p_in, p_out, owner_row, slot_row)


def prepare(recv_rows, recv_slot, turned, codes):
    owners, capacity, full = recv_rows.shape
    total = owners * capacity
    group = LANES // capacity
    rows = recv_rows[...].reshape(total, full)
    for part in range(total // LANES):
        span = slice(part * LANES, (part + 1) * LANES)
        turned[:, span] = rows[span].T
        code = recv_slot[part * group]
        for source in range(part * group + 1, (part + 1) * group):
            code = code + recv_slot[source]
        codes[:, span] = code


def query_group(step, recv_rows, turned, codes, flat, out):
    owners, capacity, full = recv_rows.shape
    width = full // 2
    row = lax.broadcasted_iota(jnp.int32, (width, full), 0)
    col = lax.broadcasted_iota(jnp.int32, (width, full), 1)
    left = col < width
    left_eye = jnp.where(row == col, 1.0, 0.0)
    right_eye = jnp.where(row + width == col, 1.0, 0.0)
    docs = range(DOC_GROUP)
    code = codes[...]
    counts, masked = [], []
    for doc in docs:
        hot = jnp.where(code == step * DOC_GROUP + doc + 1, 1.0, 0.0)
        counts.append(jnp.sum(hot, axis=1, keepdims=True))
        masked.append(turned[...] * hot.astype(BF16))
    rows = recv_rows[...].reshape(owners * capacity, full)
    half = DOC_GROUP // 2
    grams = [
        matmul(jnp.concatenate(masked[at:at + half], axis=0), rows) for at in (0, half)
    ]
    crossed, states = [], []
    for doc in docs:
        gram = grams[doc // half][doc % half * full:(doc % half + 1) * full]
        top, bottom = gram[:width], gram[width:]
        crossed.append(top)
        pair = []
        for outer in (top, pltpu.roll(bottom, width, 1)):
            damped = jnp.where(left, outer / (counts[doc] + 1.0), 0.0) + left_eye
            sums = jnp.sum(jnp.abs(damped), axis=1, keepdims=True)
            scale = 1.0 / jnp.max(sums, axis=0, keepdims=True)
            pair.append(left_eye - damped * scale + right_eye * scale)
        states.append(pair)
    for level in range(NEWTON_STEPS):
        for doc in docs:
            products = pair_product(states[doc], states[doc], False)
            states[doc] = [
                product + jnp.where(left, 0.0, state)
                for product, state in zip(products, states[doc])
            ]
    for doc in range(0, DOC_GROUP, 2):
        pair = (doc, doc + 1)
        tilted = pair_product(
            [states[d][0] for d in pair], [crossed[d] for d in pair], True)
        tilted = pair_product(tilted, [states[d][1] for d in pair], True)
        for d, value in zip(pair, tilted):
            flat[d * width:(d + 1) * width, :] = value

    near = lax.broadcasted_iota(jnp.int32, (DOC_GROUP, full), 1) < width
    for pair in range(width // 2):
        even = flat[pl.ds(2 * pair, DOC_GROUP, stride=width), :]
        odd = flat[pl.ds(2 * pair + 1, DOC_GROUP, stride=width), :]
        both = jnp.where(near, pltpu.roll(even, width, 1), odd)
        out[:, pair * full:(pair + 1) * full] = both.astype(BF16)


def query_scratch(recv_rows):
    owners, capacity, full = recv_rows.shape
    total = owners * capacity
    return [
        pltpu.VMEM((full, total), BF16),
        pltpu.VMEM((1, total), jnp.int32),
        pltpu.VMEM((DOC_GROUP * (full // 2), full), F32),
    ]


def queries_kernel(recv_rows, recv_slot, out, turned, codes, flat):
    prepare(recv_rows, recv_slot, turned, codes)

    @pl.loop(0, GROUPS)
    def _(step):
        query_group(step, recv_rows, turned, codes, flat, out.at[step])


def make_queries(recv_rows, recv_slot):
    width = recv_rows.shape[2] // 2
    return pl.pallas_call(
        queries_kernel,
        out_shape=jax.ShapeDtypeStruct((GROUPS, DOC_GROUP, width * width), BF16),
        in_specs=[VMEM_SPEC] * 2,
        out_specs=VMEM_SPEC,
        scratch_shapes=query_scratch(recv_rows),
        name="queries",
    )(recv_rows, recv_slot).reshape(DOC_DEV, width * width)


def score_into(out, index, block, train):
    out[index] = lax.dot_general(
        block[...], train[...], CONTRACT_LAST, preferred_element_type=F32
    ).astype(BF16)


def window_kernel(owners, queries, train, out, held, sent, here):
    me = lax.axis_index("blk")
    barrier = pltpu.get_barrier_semaphore()

    def peer(stop):
        return lax.rem(me + stop - LEAD + owners, owners)

    def source(stop):
        return lax.rem(me - stop + LEAD + owners, owners)

    def copy(stop):
        return pltpu.make_async_remote_copy(
            src_ref=queries, dst_ref=held.at[stop], send_sem=sent.at[stop],
            recv_sem=here.at[stop], device_id={"blk": peer(stop)}, device_id_type=MESH)

    others = [stop for stop in range(STOPS) if stop != LEAD]
    for stop in others:
        pl.semaphore_signal(
            barrier, inc=1, device_id={"blk": source(stop)}, device_id_type=MESH
        )
    pl.semaphore_wait(barrier, len(others))
    for stop in others:
        copy(stop).start()
    score_into(out, LEAD, queries, train)
    for stop in others:
        copy(stop).wait_recv()
        score_into(out, stop, held.at[stop], train)
    for stop in others:
        copy(stop).wait_send()


def grid_kernel(owners, recv_rows, recv_slot, train_far, out, turned, codes, flat, train, fetched, held,
                sent, here):
    line_size = 4
    me = lax.axis_index("blk")
    core = lax.rem(me, 2)
    side = lax.rem(me // 2, 2)
    line = me // line_size
    to_twin, to_across = 1 - 2 * core, 2 - 4 * side
    twin, across = me + to_twin, me + to_across
    above = lax.rem(me + line_size, owners)
    below = lax.rem(me + owners - line_size, owners)
    beyond = lax.rem(me + 2 * line_size, owners)

    barrier = pltpu.get_barrier_semaphore()
    for device in (twin, across, above, below, beyond):
        pl.semaphore_signal(barrier, inc=1, device_id={"blk": device}, device_id_type=MESH)
    fetch = pltpu.make_async_copy(train_far, train, fetched)
    fetch.start()
    prepare(recv_rows, recv_slot, turned, codes)

    def wrapped(stop):
        return stop % owners if isinstance(stop, int) else lax.rem(stop + 3 * owners, owners)

    def wanted(stop):
        return wrapped(stop) < STOPS

    def when(wish, act):
        if wish is True:
            act()
        else:
            pl.when(wish)(act)

    def skips(some_core):
        return (side == 0) & (some_core == 1) & (line != 1)

    left = side == 0
    own, plus, minus = LEAD, LEAD - line_size, LEAD + line_size
    beside, beside_plus, beside_minus = (LEAD - to_across + turn for turn in (0, -line_size, line_size))
    cross = LEAD - to_across - 2 * line_size
    has_plus = jnp.logical_not(skips(core))
    gives_plus = jnp.logical_not((side == 1) & (core == 1) & (line != 1))
    twin_plus = jnp.logical_not(skips(1 - core))
    has_cross = left | (core == 0)
    twin_cross = left | (core == 1)
    turns = ((side == 1) & (core == 0)) | (left & ((line == 0) | (line == 3)))

    stages = (
        (
            (own, None, ((True, above, 0), (True, below, 1), (True, across, 2), (True, twin, 3))),
        ),
        (
            (plus, True, ((gives_plus, across, 4), (True, twin, 5))),
            (minus, True, ((True, across, 6), (True, twin, 7))),
            (beside, True, ((turns, beyond, 8), (wanted(beside + to_twin), twin, 9))),
        ),
        (
            (beside_plus, has_plus, ((left & (line == 1), below, 10),
                                     (has_plus & wanted(beside_plus + to_twin), twin, 11))),
            (beside_minus, True, ((left & (line == 2), above, 12),
                                  (wanted(beside_minus + to_twin), twin, 13))),
        ),
        (
            (cross, has_cross, ((has_cross & wanted(cross + to_twin), twin, 14),)),
        ),
    )
    from_twin = (
        (own, True), (plus, True), (minus, True), (beside, True), (beside_plus, twin_plus),
        (beside_minus, True), (cross, twin_cross),
    )

    def copy(group, mine, sem, device):
        theirs = wrapped(mine + device - me)
        return pltpu.make_async_remote_copy(
            src_ref=held.at[group, wrapped(mine)], dst_ref=held.at[group, theirs],
            send_sem=sent.at[sem, group], recv_sem=here.at[group, theirs],
            device_id={"blk": device}, device_id_type=MESH)

    def arrive(group, mine):
        pltpu.make_async_remote_copy(
            src_ref=held.at[group, wrapped(mine)], dst_ref=held.at[group, wrapped(mine)],
            send_sem=sent.at[0, group], recv_sem=here.at[group, wrapped(mine)],
            device_id={"blk": twin}, device_id_type=MESH).wait_recv()

    def run(group, stage):
        for mine, comes, hands in stages[stage]:
            if comes is not None:
                when(comes, lambda: arrive(group, mine))
            for wish, device, sem in hands:
                when(wish, lambda: copy(group, mine, sem, device).start())

    last = len(stages)

    @pl.loop(0, GROUPS + last)
    def _(step):
        @pl.when(step < GROUPS)
        def _():
            query_group(step, recv_rows, turned, codes, flat, held.at[step, own])

            @pl.when(step == 0)
            def _():
                pl.semaphore_wait(barrier, 5)

            run(step, 0)

        for stage in range(1, last):
            group = step - stage

            @pl.when((group >= 0) & (group < GROUPS))
            def _():
                run(group, stage)

        @pl.when(step >= last)
        def _():
            group = step - last
            for mine, comes in from_twin:
                slot = mine - to_twin
                wish = wanted(slot) if comes is True else comes & wanted(slot)
                when(wish, lambda: arrive(group, slot))
            pl.when(group == 0)(fetch.wait)
            block = held[group, :STOPS].reshape(STOPS * DOC_GROUP, train.shape[1])
            tile = lax.dot_general(block, train[...], CONTRACT_LAST, preferred_element_type=F32)
            out[group] = tile.astype(BF16).reshape(STOPS, DOC_GROUP, train.shape[0])

    @pl.loop(0, GROUPS)
    def _(group):
        for items in stages:
            for mine, _, hands in items:
                for wish, device, sem in hands:
                    when(wish, lambda: copy(group, mine, sem, device).wait_send())


def influence_of(recv_rows, recv_slot, train):
    owners = lax.axis_size("blk")
    params = pltpu.CompilerParams(collective_id=1, has_side_effects=True)
    if owners == 16:
        tiles = pl.pallas_call(
            functools.partial(grid_kernel, owners),
            out_shape=jax.ShapeDtypeStruct((GROUPS, STOPS, DOC_GROUP, train.shape[0]), BF16),
            in_specs=[VMEM_SPEC, VMEM_SPEC, pl.BlockSpec(memory_space=pl.ANY)],
            out_specs=VMEM_SPEC,
            scratch_shapes=query_scratch(recv_rows)
            + [pltpu.VMEM(train.shape, BF16), pltpu.SemaphoreType.DMA]
            + [pltpu.VMEM((GROUPS, owners, DOC_GROUP, train.shape[1]), BF16)]
            + [pltpu.SemaphoreType.DMA((15, GROUPS)), pltpu.SemaphoreType.DMA((GROUPS, owners))],
            compiler_params=params,
            name="influence",
        )(recv_rows, recv_slot, train)
        return tiles.transpose(1, 0, 2, 3).reshape(STOPS, DOC_DEV, train.shape[0])
    queries = make_queries(recv_rows, recv_slot)
    return pl.pallas_call(
        functools.partial(window_kernel, owners),
        out_shape=jax.ShapeDtypeStruct((STOPS, DOC_DEV, train.shape[0]), BF16),
        in_specs=[VMEM_SPEC] * 2,
        out_specs=VMEM_SPEC,
        scratch_shapes=[pltpu.VMEM((STOPS,) + queries.shape, BF16)]
        + [pltpu.SemaphoreType.DMA((STOPS,))] * 2,
        compiler_params=params,
        name="influence",
    )(queries, train)


def local(query_inputs, query_grads, proj_in, proj_out, train_rows, token_owner, token_slot):
    recv_rows, recv_slot = dispatch(
        query_inputs, query_grads, proj_in.T, proj_out.T,
        token_owner.reshape(1, -1), token_slot.reshape(1, -1),
    )
    return influence_of(recv_rows, recv_slot, train_rows)


def solution(mesh):
    placed = (
        P(("groups", "blk"), None),
        P(("groups", "blk"), None),
        P(),
        P(),
        P(("groups", "blk"), None),
        P(("groups", "blk"), None),
        P(("groups", "blk")),
    )
    return jax.shard_map(
        local,
        mesh=mesh,
        in_specs=placed,
        out_specs=P(None, None, ("groups", "blk")),
        check_vma=False,
    )
```

```python
import functools

import jax
import jax.numpy as jnp
from jax import lax
from jax.experimental import pallas as pl
from jax.experimental.pallas import tpu as pltpu
from jax.sharding import PartitionSpec as P

DOC_DEV = 32
STOPS = 12
NEWTON_STEPS = 6
LEAD = 5
LANES = 128
DOC_GROUP = 8
GROUPS = DOC_DEV // DOC_GROUP
MESH = pl.DeviceIdType.MESH
VMEM_SPEC = pl.BlockSpec(memory_space=pltpu.VMEM)
FAR_SPEC = pl.BlockSpec(memory_space=pl.ANY)
F32 = jnp.float32
BF16 = jnp.bfloat16
CONTRACT_LAST = (((1,), (1,)), ((), ()))


def matmul(left, right):
    return jnp.dot(left, right, preferred_element_type=F32)


def halves(value):
    high = value.astype(BF16)
    return high, (value - high.astype(F32)).astype(BF16)


def left_parts(value, right_half):
    width = value.shape[1] // 2
    high = value.astype(BF16).astype(F32)
    low = value - high
    if right_half:
        high = pltpu.roll(high, width, 1)
    else:
        low = pltpu.roll(low, width, 1)
    is_left = lax.broadcasted_iota(jnp.int32, value.shape, 1) < width
    parts = jnp.where(is_left, high, low).astype(BF16)
    return jnp.concatenate([parts, parts], axis=1)


def pair_product(lefts, rights, right_half):
    high, low = zip(*[halves(value) for value in rights])
    high, low = jnp.concatenate(high, axis=1), jnp.concatenate(low, axis=1)
    product = matmul(
        jnp.concatenate([left_parts(value, right_half) for value in lefts], axis=0),
        jnp.concatenate([high, high, low, low], axis=0),
    )
    rows, cols = lefts[0].shape
    return product[:rows, :cols], product[rows:, cols:]


def pack(owners, capacity, owner_row, slot_row, send_slot, me):
    count = owner_row.shape[1]
    token = lax.broadcasted_iota(jnp.int32, (count, count), 0)
    other = lax.broadcasted_iota(jnp.int32, (count, count), 1)
    earlier = jnp.where(token < other, 1.0, 0.0).astype(BF16)
    owner_id = lax.broadcasted_iota(jnp.int32, (owners, count), 0)
    owner_hot = jnp.where(owner_id == owner_row[...], 1.0, 0.0)
    before = matmul(owner_hot.astype(BF16), earlier)
    rank = jnp.sum(before * owner_hot, axis=0, keepdims=True).astype(jnp.int32)
    position = owner_row[...] * capacity + rank
    place = lax.broadcasted_iota(jnp.int32, (owners * capacity, count), 0)
    placed = jnp.where(place == position, 1.0, 0.0).astype(BF16)
    coded = jnp.where(owner_id == owner_row[...], slot_row[...] + 1, 0).astype(F32).astype(BF16)
    lane = lax.broadcasted_iota(jnp.int32, (LANES, count), 0)
    shift = lax.rem(me, LANES // capacity) * capacity
    spread = jnp.where(lane == rank + shift, 1.0, 0.0).astype(BF16)
    codes = lax.dot_general(coded, spread, CONTRACT_LAST, preferred_element_type=F32)
    codes = codes.astype(jnp.int32)
    for owner in range(owners):
        send_slot[owner] = codes[owner:owner + 1]
    return placed


def greet_all(owners, me):
    barrier = pltpu.get_barrier_semaphore()

    @pl.loop(1, owners)
    def _(ahead):
        pl.semaphore_signal(
            barrier, inc=1, device_id={"blk": lax.rem(me + ahead, owners)}, device_id_type=MESH
        )

    return barrier


def exchange(owners, me, barrier, send_rows, send_slot, recv_rows, recv_slot,
             rows_sent, rows_here, slot_sent, slot_here):
    pl.semaphore_wait(barrier, owners - 1)

    def copies(target, source, sem):
        to = {"blk": target}
        return (
            pltpu.make_async_remote_copy(
                src_ref=send_rows.at[target], dst_ref=recv_rows.at[source],
                send_sem=rows_sent.at[target], recv_sem=rows_here.at[sem],
                device_id=to, device_id_type=MESH),
            pltpu.make_async_remote_copy(
                src_ref=send_slot.at[target], dst_ref=recv_slot.at[source],
                send_sem=slot_sent.at[target], recv_sem=slot_here.at[sem],
                device_id=to, device_id_type=MESH),
        )

    @pl.loop(1, owners)
    def _(ahead):
        for copy in copies(lax.rem(me + ahead, owners), me, me):
            copy.start()

    recv_rows[me] = send_rows[me]
    recv_slot[me] = send_slot[me]

    @pl.loop(1, owners)
    def _(ahead):
        source = lax.rem(me + ahead, owners)
        for copy in copies(source, source, source):
            copy.wait_recv()

    def drain():
        @pl.loop(1, owners)
        def _(ahead):
            for copy in copies(lax.rem(me + ahead, owners), me, me):
                copy.wait_send()

    return drain


def gather(owners, capacity, far, near, fetched, low, send_rows, send_slot, recv_rows, recv_slot,
           rows_sent, rows_here, slot_sent, slot_here):
    me = lax.axis_index("blk")
    fetches = [pltpu.make_async_copy(*pair, fetched.at[i]) for i, pair in enumerate(zip(far, near))]
    for fetch in fetches:
        fetch.start()
    barrier = greet_all(owners, me)
    owner_row, slot_row, p_out, x_grad, p_in, x_in = near
    width = p_in.shape[0]
    for fetch in fetches[:2]:
        fetch.wait()
    placed = pack(owners, capacity, owner_row, slot_row, send_slot, me)
    for at, values, weights, waits in (
        (0, x_grad, p_out, fetches[2:4]), (width, x_in, p_in, fetches[4:6])
    ):
        for fetch in waits:
            fetch.wait()
        low[:, at:at + width] = lax.dot_general(
            values[...], weights[...], CONTRACT_LAST, preferred_element_type=F32
        ).astype(BF16)
    send_rows[...] = matmul(placed, low[...]).astype(BF16).reshape(send_rows.shape)
    return exchange(owners, me, barrier, send_rows, send_slot, recv_rows, recv_slot,
                    rows_sent, rows_here, slot_sent, slot_here)


def dispatch_kernel(owners, capacity, *refs):
    far, (recv_rows, recv_slot), near, rest = refs[:6], refs[6:8], refs[8:14], refs[14:]
    drain = gather(owners, capacity, far, near, *rest[:4], recv_rows, recv_slot, *rest[4:])
    drain()


def gather_scratch(owners, capacity, near):
    count, width = near[3].shape[0], near[2].shape[0]
    return [pltpu.VMEM(item.shape, item.dtype) for item in near] + [
        pltpu.SemaphoreType.DMA((len(near),)),
        pltpu.VMEM((count, 2 * width), BF16),
        pltpu.VMEM((owners, capacity, 2 * width), BF16),
        pltpu.VMEM((owners, 1, LANES), jnp.int32),
    ]


def dispatch(owners, capacity, inputs):
    width = inputs[2].shape[0]
    rows = (owners, capacity, 2 * width)
    slots = (owners, 1, LANES)
    return pl.pallas_call(
        functools.partial(dispatch_kernel, owners, capacity),
        out_shape=(jax.ShapeDtypeStruct(rows, BF16), jax.ShapeDtypeStruct(slots, jnp.int32)),
        in_specs=[FAR_SPEC] * len(inputs),
        out_specs=(VMEM_SPEC, VMEM_SPEC),
        scratch_shapes=gather_scratch(owners, capacity, inputs)
        + [pltpu.SemaphoreType.DMA((owners,))] * 4,
        compiler_params=pltpu.CompilerParams(collective_id=0, has_side_effects=True),
        name="dispatch",
    )(*inputs)


def prepare(recv_rows, recv_slot, turned, codes):
    owners, capacity, full = recv_rows.shape
    total = owners * capacity
    group = LANES // capacity
    rows = recv_rows[...].reshape(total, full)
    for part in range(total // LANES):
        span = slice(part * LANES, (part + 1) * LANES)
        turned[:, span] = rows[span].T
        code = recv_slot[part * group]
        for source in range(part * group + 1, (part + 1) * group):
            code = code + recv_slot[source]
        codes[:, span] = code


def query_group(step, recv_rows, turned, codes, flat, out):
    owners, capacity, full = recv_rows.shape
    width = full // 2
    row = lax.broadcasted_iota(jnp.int32, (width, full), 0)
    col = lax.broadcasted_iota(jnp.int32, (width, full), 1)
    left = col < width
    left_eye = jnp.where(row == col, 1.0, 0.0)
    right_eye = jnp.where(row + width == col, 1.0, 0.0)
    docs = range(DOC_GROUP)
    code = codes[...]
    counts, masked = [], []
    for doc in docs:
        hot = jnp.where(code == step * DOC_GROUP + doc + 1, 1.0, 0.0)
        counts.append(jnp.sum(hot, axis=1, keepdims=True))
        masked.append(turned[...] * hot.astype(BF16))
    rows = recv_rows[...].reshape(owners * capacity, full)
    half = DOC_GROUP // 2
    grams = [
        matmul(jnp.concatenate(masked[at:at + half], axis=0), rows) for at in (0, half)
    ]
    crossed, states = [], []
    for doc in docs:
        gram = grams[doc // half][doc % half * full:(doc % half + 1) * full]
        top, bottom = gram[:width], gram[width:]
        crossed.append(top)
        pair = []
        for outer in (top, pltpu.roll(bottom, width, 1)):
            damped = jnp.where(left, outer / (counts[doc] + 1.0), 0.0) + left_eye
            sums = jnp.sum(jnp.abs(damped), axis=1, keepdims=True)
            scale = 1.0 / jnp.max(sums, axis=0, keepdims=True)
            pair.append(left_eye - damped * scale + right_eye * scale)
        states.append(pair)
    for level in range(NEWTON_STEPS):
        for doc in docs:
            products = pair_product(states[doc], states[doc], False)
            states[doc] = [
                product + jnp.where(left, 0.0, state)
                for product, state in zip(products, states[doc])
            ]
    for doc in range(0, DOC_GROUP, 2):
        pair = (doc, doc + 1)
        tilted = pair_product(
            [states[d][0] for d in pair], [crossed[d] for d in pair], True)
        tilted = pair_product(tilted, [states[d][1] for d in pair], True)
        for d, value in zip(pair, tilted):
            flat[d * width:(d + 1) * width, :] = value

    near = lax.broadcasted_iota(jnp.int32, (DOC_GROUP, full), 1) < width
    for pair in range(width // 2):
        even = flat[pl.ds(2 * pair, DOC_GROUP, stride=width), :]
        odd = flat[pl.ds(2 * pair + 1, DOC_GROUP, stride=width), :]
        both = jnp.where(near, pltpu.roll(even, width, 1), odd)
        out[:, pair * full:(pair + 1) * full] = both.astype(BF16)


def query_scratch(recv_rows):
    owners, capacity, full = recv_rows.shape
    total = owners * capacity
    return [
        pltpu.VMEM((full, total), BF16),
        pltpu.VMEM((1, total), jnp.int32),
        pltpu.VMEM((DOC_GROUP * (full // 2), full), F32),
    ]


def queries_kernel(recv_rows, recv_slot, out, turned, codes, flat):
    prepare(recv_rows, recv_slot, turned, codes)

    @pl.loop(0, GROUPS)
    def _(step):
        query_group(step, recv_rows, turned, codes, flat, out.at[step])


def make_queries(recv_rows, recv_slot):
    width = recv_rows.shape[2] // 2
    return pl.pallas_call(
        queries_kernel,
        out_shape=jax.ShapeDtypeStruct((GROUPS, DOC_GROUP, width * width), BF16),
        in_specs=[VMEM_SPEC] * 2,
        out_specs=VMEM_SPEC,
        scratch_shapes=query_scratch(recv_rows),
        name="queries",
    )(recv_rows, recv_slot).reshape(DOC_DEV, width * width)


def score_into(out, index, block, train):
    out[index] = lax.dot_general(
        block[...], train[...], CONTRACT_LAST, preferred_element_type=F32
    ).astype(BF16)


def window_kernel(owners, queries, train, out, held, sent, here):
    me = lax.axis_index("blk")
    barrier = pltpu.get_barrier_semaphore()

    def peer(stop):
        return lax.rem(me + stop - LEAD + owners, owners)

    def source(stop):
        return lax.rem(me - stop + LEAD + owners, owners)

    def copy(stop):
        return pltpu.make_async_remote_copy(
            src_ref=queries, dst_ref=held.at[stop], send_sem=sent.at[stop],
            recv_sem=here.at[stop], device_id={"blk": peer(stop)}, device_id_type=MESH)

    others = [stop for stop in range(STOPS) if stop != LEAD]
    for stop in others:
        pl.semaphore_signal(
            barrier, inc=1, device_id={"blk": source(stop)}, device_id_type=MESH
        )
    pl.semaphore_wait(barrier, len(others))
    for stop in others:
        copy(stop).start()
    score_into(out, LEAD, queries, train)
    for stop in others:
        copy(stop).wait_recv()
        score_into(out, stop, held.at[stop], train)
    for stop in others:
        copy(stop).wait_send()


def grid_kernel(owners, capacity, *refs):
    far, train_far, out, near = refs[:6], refs[6], refs[7], refs[8:14]
    got, low, send_rows, send_slot, recv_rows, recv_slot = refs[14:20]
    rows_sent, rows_here, slot_sent, slot_here = refs[20:24]
    turned, codes, flat, train, fetched, held, sent, here = refs[24:]
    line_size = 4
    me = lax.axis_index("blk")
    core = lax.rem(me, 2)
    side = lax.rem(me // 2, 2)
    line = me // line_size
    to_twin, to_across = 1 - 2 * core, 2 - 4 * side
    twin, across = me + to_twin, me + to_across
    above = lax.rem(me + line_size, owners)
    below = lax.rem(me + owners - line_size, owners)
    beyond = lax.rem(me + 2 * line_size, owners)

    drain = gather(owners, capacity, far, near, got, low, send_rows, send_slot, recv_rows, recv_slot,
                   rows_sent, rows_here, slot_sent, slot_here)
    fetch = pltpu.make_async_copy(train_far, train, fetched)
    fetch.start()
    prepare(recv_rows, recv_slot, turned, codes)

    def wrapped(stop):
        return stop % owners if isinstance(stop, int) else lax.rem(stop + 3 * owners, owners)

    def wanted(stop):
        return wrapped(stop) < STOPS

    def when(wish, act):
        if wish is True:
            act()
        else:
            pl.when(wish)(act)

    def skips(some_core):
        return (side == 0) & (some_core == 1) & (line != 1)

    left = side == 0
    own, plus, minus = LEAD, LEAD - line_size, LEAD + line_size
    beside, beside_plus, beside_minus = (LEAD - to_across + turn for turn in (0, -line_size, line_size))
    cross = LEAD - to_across - 2 * line_size
    has_plus = jnp.logical_not(skips(core))
    gives_plus = jnp.logical_not((side == 1) & (core == 1) & (line != 1))
    twin_plus = jnp.logical_not(skips(1 - core))
    has_cross = left | (core == 0)
    twin_cross = left | (core == 1)
    turns = ((side == 1) & (core == 0)) | (left & ((line == 0) | (line == 3)))

    stages = (
        (
            (own, None, ((True, above, 0), (True, below, 1), (True, across, 2), (True, twin, 3))),
        ),
        (
            (plus, True, ((gives_plus, across, 4), (True, twin, 5))),
            (minus, True, ((True, across, 6), (True, twin, 7))),
            (beside, True, ((turns, beyond, 8), (wanted(beside + to_twin), twin, 9))),
        ),
        (
            (beside_plus, has_plus, ((left & (line == 1), below, 10),
                                     (has_plus & wanted(beside_plus + to_twin), twin, 11))),
            (beside_minus, True, ((left & (line == 2), above, 12),
                                  (wanted(beside_minus + to_twin), twin, 13))),
        ),
        (
            (cross, has_cross, ((has_cross & wanted(cross + to_twin), twin, 14),)),
        ),
    )
    from_twin = (
        (own, True), (plus, True), (minus, True), (beside, True), (beside_plus, twin_plus),
        (beside_minus, True), (cross, twin_cross),
    )

    def copy(group, mine, sem, device):
        theirs = wrapped(mine + device - me)
        return pltpu.make_async_remote_copy(
            src_ref=held.at[group, wrapped(mine)], dst_ref=held.at[group, theirs],
            send_sem=sent.at[sem, group], recv_sem=here.at[group, theirs],
            device_id={"blk": device}, device_id_type=MESH)

    def arrive(group, mine):
        pltpu.make_async_remote_copy(
            src_ref=held.at[group, wrapped(mine)], dst_ref=held.at[group, wrapped(mine)],
            send_sem=sent.at[0, group], recv_sem=here.at[group, wrapped(mine)],
            device_id={"blk": twin}, device_id_type=MESH).wait_recv()

    def run(group, stage):
        for mine, comes, hands in stages[stage]:
            if comes is not None:
                when(comes, lambda: arrive(group, mine))
            for wish, device, sem in hands:
                when(wish, lambda: copy(group, mine, sem, device).start())

    last = len(stages)

    @pl.loop(0, GROUPS + last)
    def _(step):
        @pl.when(step < GROUPS)
        def _():
            query_group(step, recv_rows, turned, codes, flat, held.at[step, own])

            run(step, 0)

        for stage in range(1, last):
            group = step - stage

            @pl.when((group >= 0) & (group < GROUPS))
            def _():
                run(group, stage)

        @pl.when(step >= last)
        def _():
            group = step - last
            for mine, comes in from_twin:
                slot = mine - to_twin
                wish = wanted(slot) if comes is True else comes & wanted(slot)
                when(wish, lambda: arrive(group, slot))
            pl.when(group == 0)(fetch.wait)
            block = held[group, :STOPS].reshape(STOPS * DOC_GROUP, train.shape[1])
            tile = lax.dot_general(block, train[...], CONTRACT_LAST, preferred_element_type=F32)
            out[group] = tile.astype(BF16).reshape(STOPS, DOC_GROUP, train.shape[0])

    @pl.loop(0, GROUPS)
    def _(group):
        for items in stages:
            for mine, _, hands in items:
                for wish, device, sem in hands:
                    when(wish, lambda: copy(group, mine, sem, device).wait_send())
    drain()


def influence_of(owners, capacity, inputs, train):
    width = inputs[2].shape[0]
    if owners == 16:
        recv_rows = jax.ShapeDtypeStruct((owners, capacity, 2 * width), BF16)
        tiles = pl.pallas_call(
            functools.partial(grid_kernel, owners, capacity),
            out_shape=jax.ShapeDtypeStruct((GROUPS, STOPS, DOC_GROUP, train.shape[0]), BF16),
            in_specs=[FAR_SPEC] * (len(inputs) + 1),
            out_specs=VMEM_SPEC,
            scratch_shapes=gather_scratch(owners, capacity, inputs)
            + [pltpu.VMEM(recv_rows.shape, BF16), pltpu.VMEM((owners, 1, LANES), jnp.int32)]
            + [pltpu.SemaphoreType.DMA((owners,))] * 4
            + query_scratch(recv_rows)
            + [pltpu.VMEM(train.shape, BF16), pltpu.SemaphoreType.DMA]
            + [pltpu.VMEM((GROUPS, owners, DOC_GROUP, train.shape[1]), BF16)]
            + [pltpu.SemaphoreType.DMA((15, GROUPS)), pltpu.SemaphoreType.DMA((GROUPS, owners))],
            compiler_params=pltpu.CompilerParams(
                collective_id=0, has_side_effects=True, vmem_limit_bytes=32 << 20),
            name="influence",
        )(*inputs, train)
        return tiles.transpose(1, 0, 2, 3).reshape(STOPS, DOC_DEV, train.shape[0])
    queries = make_queries(*dispatch(owners, capacity, inputs))
    return pl.pallas_call(
        functools.partial(window_kernel, owners),
        out_shape=jax.ShapeDtypeStruct((STOPS, DOC_DEV, train.shape[0]), BF16),
        in_specs=[VMEM_SPEC] * 2,
        out_specs=VMEM_SPEC,
        scratch_shapes=[pltpu.VMEM((STOPS,) + queries.shape, BF16)]
        + [pltpu.SemaphoreType.DMA((STOPS,))] * 2,
        compiler_params=pltpu.CompilerParams(collective_id=1, has_side_effects=True),
        name="influence",
    )(queries, train)


def local(query_inputs, query_grads, proj_in, proj_out, train_rows, token_owner, token_slot):
    owners = lax.axis_size("blk")
    inputs = (
        token_owner.reshape(1, -1), token_slot.reshape(1, -1),
        proj_out.T, query_grads, proj_in.T, query_inputs, train_rows,
    )
    *inputs, train = [pltpu.with_memory_space_constraint(item, pltpu.HBM) for item in inputs]
    return influence_of(owners, 4 * query_inputs.shape[0] // owners, inputs, train)


def solution(mesh):
    placed = (
        P(("groups", "blk"), None),
        P(("groups", "blk"), None),
        P(),
        P(),
        P(("groups", "blk"), None),
        P(("groups", "blk"), None),
        P(("groups", "blk")),
    )
    return jax.shard_map(
        local,
        mesh=mesh,
        in_specs=placed,
        out_specs=P(None, None, ("groups", "blk")),
        check_vma=False,
    )
```

```python
import functools

import jax
import jax.numpy as jnp
from jax import lax
from jax.experimental import pallas as pl
from jax.experimental.pallas import tpu as pltpu
from jax.sharding import PartitionSpec as P

DOC_DEV = 32
STOPS = 12
NEWTON_STEPS = 6
LEAD = 5
CUT = 2
FLIP = 4
LANES = 128
DOC_GROUP = 8
GROUPS = DOC_DEV // DOC_GROUP
MESH = pl.DeviceIdType.MESH
VMEM_SPEC = pl.BlockSpec(memory_space=pltpu.VMEM)
FAR_SPEC = pl.BlockSpec(memory_space=pl.ANY)
F32 = jnp.float32
BF16 = jnp.bfloat16
CONTRACT_LAST = (((1,), (1,)), ((), ()))


def matmul(left, right):
    return jnp.dot(left, right, preferred_element_type=F32)


def halves(value):
    high = value.astype(BF16)
    return high, (value - high.astype(F32)).astype(BF16)


def pack(owners, capacity, owner_row, slot_row, send_slot, me):
    count = owner_row.shape[1]
    token = lax.broadcasted_iota(jnp.int32, (count, count), 0)
    other = lax.broadcasted_iota(jnp.int32, (count, count), 1)
    earlier = jnp.where(token < other, 1.0, 0.0).astype(BF16)
    owner_id = lax.broadcasted_iota(jnp.int32, (owners, count), 0)
    owner_hot = jnp.where(owner_id == owner_row[...], 1.0, 0.0)
    before = matmul(owner_hot.astype(BF16), earlier)
    rank = jnp.sum(before * owner_hot, axis=0, keepdims=True).astype(jnp.int32)
    position = owner_row[...] * capacity + rank
    place = lax.broadcasted_iota(jnp.int32, (owners * capacity, count), 0)
    placed = jnp.where(place == position, 1.0, 0.0).astype(BF16)
    coded = jnp.where(owner_id == owner_row[...], slot_row[...] + 1, 0).astype(F32).astype(BF16)
    lane = lax.broadcasted_iota(jnp.int32, (LANES, count), 0)
    shift = lax.rem(me, LANES // capacity) * capacity
    spread = jnp.where(lane == rank + shift, 1.0, 0.0).astype(BF16)
    codes = lax.dot_general(coded, spread, CONTRACT_LAST, preferred_element_type=F32)
    codes = codes.astype(jnp.int32)
    for owner in range(owners):
        send_slot[owner] = codes[owner:owner + 1]
    return placed


def greet_all(owners, me):
    barrier = pltpu.get_barrier_semaphore()

    @pl.loop(1, owners)
    def _(ahead):
        pl.semaphore_signal(
            barrier, inc=1, device_id={"blk": lax.rem(me + ahead, owners)}, device_id_type=MESH
        )

    return barrier


def exchange(owners, me, barrier, send_rows, send_slot, recv_rows, recv_slot,
             rows_sent, rows_here, slot_sent, slot_here, during):
    pl.semaphore_wait(barrier, owners - 1)

    def copies(target, source, sem):
        to = {"blk": target}
        return (
            pltpu.make_async_remote_copy(
                src_ref=send_rows.at[target], dst_ref=recv_rows.at[source],
                send_sem=rows_sent.at[target], recv_sem=rows_here.at[sem],
                device_id=to, device_id_type=MESH),
            pltpu.make_async_remote_copy(
                src_ref=send_slot.at[target], dst_ref=recv_slot.at[source],
                send_sem=slot_sent.at[target], recv_sem=slot_here.at[sem],
                device_id=to, device_id_type=MESH),
        )

    @pl.loop(1, owners)
    def _(ahead):
        for copy in copies(lax.rem(me + ahead, owners), me, me):
            copy.start()

    recv_rows[me] = send_rows[me]
    recv_slot[me] = send_slot[me]
    if during is not None:
        during()

    @pl.loop(1, owners)
    def _(ahead):
        source = lax.rem(me + ahead, owners)
        for copy in copies(source, source, source):
            copy.wait_recv()

    def drain():
        @pl.loop(1, owners)
        def _(ahead):
            for copy in copies(lax.rem(me + ahead, owners), me, me):
                copy.wait_send()

    return drain


def gather(owners, capacity, far, near, fetched, low, send_rows, send_slot, recv_rows, recv_slot,
           rows_sent, rows_here, slot_sent, slot_here, during=None):
    me = lax.axis_index("blk")
    fetches = [pltpu.make_async_copy(*pair, fetched.at[i]) for i, pair in enumerate(zip(far, near))]
    for fetch in fetches:
        fetch.start()
    barrier = greet_all(owners, me)
    owner_row, slot_row, p_out, x_grad, p_in, x_in = near
    width = p_in.shape[0]
    for fetch in fetches[:2]:
        fetch.wait()
    placed = pack(owners, capacity, owner_row, slot_row, send_slot, me)
    for at, values, weights, waits in (
        (0, x_grad, p_out, fetches[2:4]), (width, x_in, p_in, fetches[4:6])
    ):
        for fetch in waits:
            fetch.wait()
        low[:, at:at + width] = lax.dot_general(
            values[...], weights[...], CONTRACT_LAST, preferred_element_type=F32
        ).astype(BF16)
    send_rows[...] = matmul(placed, low[...]).astype(BF16).reshape(send_rows.shape)
    return exchange(owners, me, barrier, send_rows, send_slot, recv_rows, recv_slot,
                    rows_sent, rows_here, slot_sent, slot_here, during)


def dispatch_kernel(owners, capacity, *refs):
    far, (recv_rows, recv_slot), near, rest = refs[:6], refs[6:8], refs[8:14], refs[14:]
    drain = gather(owners, capacity, far, near, *rest[:4], recv_rows, recv_slot, *rest[4:])
    drain()


def gather_scratch(owners, capacity, near):
    count, width = near[3].shape[0], near[2].shape[0]
    return [pltpu.VMEM(item.shape, item.dtype) for item in near] + [
        pltpu.SemaphoreType.DMA((len(near),)),
        pltpu.VMEM((count, 2 * width), BF16),
        pltpu.VMEM((owners, capacity, 2 * width), BF16),
        pltpu.VMEM((owners, 1, LANES), jnp.int32),
    ]


def dispatch(owners, capacity, inputs):
    width = inputs[2].shape[0]
    rows = (owners, capacity, 2 * width)
    slots = (owners, 1, LANES)
    return pl.pallas_call(
        functools.partial(dispatch_kernel, owners, capacity),
        out_shape=(jax.ShapeDtypeStruct(rows, BF16), jax.ShapeDtypeStruct(slots, jnp.int32)),
        in_specs=[FAR_SPEC] * len(inputs),
        out_specs=(VMEM_SPEC, VMEM_SPEC),
        scratch_shapes=gather_scratch(owners, capacity, inputs)
        + [pltpu.SemaphoreType.DMA((owners,))] * 4,
        compiler_params=pltpu.CompilerParams(collective_id=0, has_side_effects=True),
        name="dispatch",
    )(*inputs)


def prepare(recv_rows, recv_slot, turned, codes):
    owners, capacity, full = recv_rows.shape
    total = owners * capacity
    group = LANES // capacity
    rows = recv_rows[...].reshape(total, full)
    for part in range(total // LANES):
        span = slice(part * LANES, (part + 1) * LANES)
        turned[:, span] = rows[span].T
        code = recv_slot[part * group]
        for source in range(part * group + 1, (part + 1) * group):
            code = code + recv_slot[source]
        codes[:, span] = code


def beside_each_other(value, left):
    high, low = halves(value)
    right = (1.0 - left.astype(F32)).astype(BF16)
    tops = jnp.concatenate([high * left, low * left], axis=1)
    bottoms = jnp.concatenate([high * right, low * right], axis=1)
    return jnp.concatenate([tops, bottoms, tops, bottoms], axis=0)


def stack(values):
    return jnp.concatenate([jnp.concatenate(halves(value), axis=1) for value in values], axis=0)


def times(lefts, weights):
    product = matmul(stack(lefts), weights)
    lanes = product.shape[1] // 2
    product = product[:, :lanes] + product[:, lanes:]
    rows = lefts[0].shape[0]
    return [product[at * rows:(at + 1) * rows] for at in range(len(lefts))]


def query_group(step, recv_rows, turned, codes, flat, out):
    owners, capacity, full = recv_rows.shape
    width = full // 2
    row = lax.broadcasted_iota(jnp.int32, (width, full), 0)
    col = lax.broadcasted_iota(jnp.int32, (width, full), 1)
    left = lax.broadcasted_iota(jnp.int32, (1, full), 1) < width
    eye = jnp.where((row == col) | (row + width == col), 1.0, 0.0)
    left_half = jnp.where(col < width, 1.0, 0.0).astype(BF16)
    docs = range(DOC_GROUP)
    code = codes[...]
    counts, masked = [], []
    for doc in docs:
        hot = jnp.where(code == step * DOC_GROUP + doc + 1, 1.0, 0.0)
        counts.append(jnp.sum(hot, axis=1, keepdims=True))
        masked.append(turned[...] * hot.astype(BF16))
    rows = recv_rows[...].reshape(owners * capacity, full)
    half = DOC_GROUP // 2
    grams = [
        matmul(jnp.concatenate(masked[at:at + half], axis=0), rows) for at in (0, half)
    ]
    states, sums = [], []
    for doc in docs:
        gram = grams[doc // half][doc % half * full:(doc % half + 1) * full]
        top, bottom = gram[:width], gram[width:]
        damped = jnp.where(left, top, bottom) / (counts[doc] + 1.0) + eye
        spread = jnp.sum(jnp.abs(damped), axis=0, keepdims=True)
        bounds = [
            jnp.max(jnp.where(side, spread, 0.0), axis=1, keepdims=True)
            for side in (left, jnp.logical_not(left))
        ]
        scale = jnp.where(left, 1.0 / bounds[0], 1.0 / bounds[1])
        states.append(eye - damped * scale)
        sums.append(jnp.where(left, eye, top) * scale)
    for level in range(NEWTON_STEPS):
        for doc in docs:
            state, total = states[doc], sums[doc]
            weights = beside_each_other(state, left_half)
            if level < NEWTON_STEPS - 1:
                states[doc], more = times([state, total], weights)
            else:
                more, = times([total], weights)
            sums[doc] = total + more
    zeros = jnp.zeros((width, 2 * full), BF16)
    for doc in docs:
        pieces = stack([sums[doc]])
        flat[doc * width:(doc + 1) * width, :], = times(
            [sums[doc]], jnp.concatenate([pieces, zeros, pieces, zeros], axis=0))
    near = lax.broadcasted_iota(jnp.int32, (DOC_GROUP, full), 1) < width
    for pair in range(width // 2):
        even = flat[pl.ds(2 * pair, DOC_GROUP, stride=width), :]
        odd = flat[pl.ds(2 * pair + 1, DOC_GROUP, stride=width), :]
        both = jnp.where(near, pltpu.roll(even, width, 1), odd)
        out[:, pair * full:(pair + 1) * full] = both.astype(BF16)


def query_scratch(recv_rows):
    owners, capacity, full = recv_rows.shape
    total = owners * capacity
    return [
        pltpu.VMEM((full, total), BF16),
        pltpu.VMEM((1, total), jnp.int32),
        pltpu.VMEM((DOC_GROUP * (full // 2), full), F32),
    ]


def queries_kernel(recv_rows, recv_slot, out, turned, codes, flat):
    prepare(recv_rows, recv_slot, turned, codes)

    @pl.loop(0, GROUPS)
    def _(step):
        query_group(step, recv_rows, turned, codes, flat, out.at[step])


def make_queries(recv_rows, recv_slot):
    width = recv_rows.shape[2] // 2
    return pl.pallas_call(
        queries_kernel,
        out_shape=jax.ShapeDtypeStruct((GROUPS, DOC_GROUP, width * width), BF16),
        in_specs=[VMEM_SPEC] * 2,
        out_specs=VMEM_SPEC,
        scratch_shapes=query_scratch(recv_rows),
        name="queries",
    )(recv_rows, recv_slot).reshape(DOC_DEV, width * width)


def score_into(out, index, block, train):
    out[index] = lax.dot_general(
        block[...], train[...], CONTRACT_LAST, preferred_element_type=F32
    ).astype(BF16)


def window_kernel(owners, queries, train, out, held, sent, here):
    me = lax.axis_index("blk")
    barrier = pltpu.get_barrier_semaphore()

    def peer(stop):
        return lax.rem(me + stop - LEAD + owners, owners)

    def source(stop):
        return lax.rem(me - stop + LEAD + owners, owners)

    def copy(stop):
        return pltpu.make_async_remote_copy(
            src_ref=queries, dst_ref=held.at[stop], send_sem=sent.at[stop],
            recv_sem=here.at[stop], device_id={"blk": peer(stop)}, device_id_type=MESH)

    others = [stop for stop in range(STOPS) if stop != LEAD]
    for stop in others:
        pl.semaphore_signal(
            barrier, inc=1, device_id={"blk": source(stop)}, device_id_type=MESH
        )
    pl.semaphore_wait(barrier, len(others))
    for stop in others:
        copy(stop).start()
    score_into(out, LEAD, queries, train)
    for stop in others:
        copy(stop).wait_recv()
        score_into(out, stop, held.at[stop], train)
    for stop in others:
        copy(stop).wait_send()


def grid_kernel(owners, capacity, *refs):
    far, train_far, out, near = refs[:6], refs[6], refs[7], refs[8:14]
    got, low, send_rows, send_slot, recv_rows, recv_slot = refs[14:20]
    rows_sent, rows_here, slot_sent, slot_here = refs[20:24]
    turned, codes, flat, train, train_turned, fetched, held, sent, here = refs[24:]
    line_size = 4
    me = lax.axis_index("blk")
    core = lax.rem(me, 2)
    side = lax.rem(me // 2, 2)
    line = me // line_size
    to_twin, to_across = 1 - 2 * core, 2 - 4 * side
    twin, across = me + to_twin, me + to_across
    above = lax.rem(me + line_size, owners)
    below = lax.rem(me + owners - line_size, owners)
    beyond = lax.rem(me + 2 * line_size, owners)

    fetch = pltpu.make_async_copy(train_far, train, fetched)

    def flip():
        fetch.start()
        fetch.wait()

        @pl.loop(0, train.shape[1] // (FLIP * LANES))
        def _(step):
            for part in range(FLIP):
                at = pl.multiple_of((step * FLIP + part) * LANES, LANES)
                train_turned[pl.ds(at, LANES), :] = train[:, pl.ds(at, LANES)].T

    drain = gather(owners, capacity, far, near, got, low, send_rows, send_slot, recv_rows, recv_slot,
                   rows_sent, rows_here, slot_sent, slot_here, flip)
    prepare(recv_rows, recv_slot, turned, codes)

    def wrapped(stop):
        return stop % owners if isinstance(stop, int) else lax.rem(stop + 3 * owners, owners)

    def wanted(stop):
        return wrapped(stop) < STOPS

    def when(wish, act):
        if wish is True:
            act()
        else:
            pl.when(wish)(act)

    def skips(some_core):
        return (side == 0) & (some_core == 1) & (line != 1)

    left = side == 0
    own, plus, minus = LEAD, LEAD - line_size, LEAD + line_size
    beside, beside_plus, beside_minus = (LEAD - to_across + turn for turn in (0, -line_size, line_size))
    cross = LEAD - to_across - 2 * line_size
    has_plus = jnp.logical_not(skips(core))
    gives_plus = jnp.logical_not((side == 1) & (core == 1) & (line != 1))
    twin_plus = jnp.logical_not(skips(1 - core))
    has_cross = left | (core == 0)
    twin_cross = left | (core == 1)

    def hands_of(group):
        late = group >= CUT
        turns = ((side == 1) & (core == 0)) | (left & ((line == 0) | (line == 3) | late))
        chains = left & jnp.logical_not(late)
        return (
            (
                (own, None, ((True, above, 0), (True, below, 1), (True, across, 2), (True, twin, 3))),
            ),
            (
                (beside, True, ((turns, beyond, 8), (wanted(beside + to_twin), twin, 9))),
            ),
            (
                (plus, True, ((gives_plus, across, 4), (True, twin, 5))),
                (minus, True, ((True, across, 6), (True, twin, 7))),
            ),
            (
                (beside_plus, has_plus, ((chains & (line == 1), below, 10),
                                         (has_plus & wanted(beside_plus + to_twin), twin, 11))),
                (beside_minus, True, ((chains & (line == 2), above, 12),
                                      (wanted(beside_minus + to_twin), twin, 13))),
            ),
            (
                (cross, has_cross, ((has_cross & wanted(cross + to_twin), twin, 14),)),
            ),
        )

    from_twin = (
        (own, True), (plus, True), (minus, True), (beside, True), (beside_plus, twin_plus),
        (beside_minus, True), (cross, twin_cross),
    )

    def copy(group, mine, sem, device):
        theirs = wrapped(mine + device - me)
        return pltpu.make_async_remote_copy(
            src_ref=held.at[group, wrapped(mine)], dst_ref=held.at[group, theirs],
            send_sem=sent.at[sem, group], recv_sem=here.at[group, theirs],
            device_id={"blk": device}, device_id_type=MESH)

    def arrive(group, mine):
        pltpu.make_async_remote_copy(
            src_ref=held.at[group, wrapped(mine)], dst_ref=held.at[group, wrapped(mine)],
            send_sem=sent.at[0, group], recv_sem=here.at[group, wrapped(mine)],
            device_id={"blk": twin}, device_id_type=MESH).wait_recv()

    def run(group, stage):
        for mine, comes, hands in hands_of(jnp.int32(group))[stage]:
            if comes is not None:
                when(comes, lambda: arrive(group, mine))
            for wish, device, sem in hands:
                when(wish, lambda: copy(group, mine, sem, device).start())

    def sent_by(group):
        for items in hands_of(jnp.int32(group)):
            for mine, _, hands in items:
                for wish, device, sem in hands:
                    when(wish, lambda: copy(group, mine, sem, device).wait_send())

    last = 4

    @pl.loop(0, GROUPS + last)
    def _(step):
        @pl.when(step < GROUPS)
        def _():
            query_group(step, recv_rows, turned, codes, flat, held.at[step, own])
            run(step, 0)
            pl.when(step == GROUPS - 1)(drain)

        for stage, lag in ((1, 1), (2, 1), (3, 2), (4, 3)):
            group = step - lag

            @pl.when((group >= 0) & (group < GROUPS))
            def _():
                run(group, stage)

        @pl.when(step >= last)
        def _():
            group = step - last
            pl.when(group > 0)(lambda: sent_by(group - 1))
            for mine, comes in from_twin:
                slot = mine - to_twin
                wish = wanted(slot) if comes is True else comes & wanted(slot)
                when(wish, lambda: arrive(group, slot))
            block = held[group, :STOPS].reshape(STOPS * DOC_GROUP, train.shape[1])
            tile = matmul(block, train_turned[...])
            out[group] = tile.astype(BF16).reshape(STOPS, DOC_GROUP, train.shape[0])

    sent_by(GROUPS - 1)


def influence_of(owners, capacity, inputs, train):
    width = inputs[2].shape[0]
    if owners == 16:
        recv_rows = jax.ShapeDtypeStruct((owners, capacity, 2 * width), BF16)
        tiles = pl.pallas_call(
            functools.partial(grid_kernel, owners, capacity),
            out_shape=jax.ShapeDtypeStruct((GROUPS, STOPS, DOC_GROUP, train.shape[0]), BF16),
            in_specs=[FAR_SPEC] * (len(inputs) + 1),
            out_specs=VMEM_SPEC,
            scratch_shapes=gather_scratch(owners, capacity, inputs)
            + [pltpu.VMEM(recv_rows.shape, BF16), pltpu.VMEM((owners, 1, LANES), jnp.int32)]
            + [pltpu.SemaphoreType.DMA((owners,))] * 4
            + query_scratch(recv_rows)
            + [pltpu.VMEM(train.shape, BF16), pltpu.VMEM(train.shape[::-1], BF16)]
            + [pltpu.SemaphoreType.DMA]
            + [pltpu.VMEM((GROUPS, owners, DOC_GROUP, train.shape[1]), BF16)]
            + [pltpu.SemaphoreType.DMA((15, GROUPS)), pltpu.SemaphoreType.DMA((GROUPS, owners))],
            compiler_params=pltpu.CompilerParams(
                collective_id=0, has_side_effects=True, vmem_limit_bytes=32 << 20),
            name="influence",
        )(*inputs, train)
        return tiles.transpose(1, 0, 2, 3).reshape(STOPS, DOC_DEV, train.shape[0])
    queries = make_queries(*dispatch(owners, capacity, inputs))
    return pl.pallas_call(
        functools.partial(window_kernel, owners),
        out_shape=jax.ShapeDtypeStruct((STOPS, DOC_DEV, train.shape[0]), BF16),
        in_specs=[VMEM_SPEC] * 2,
        out_specs=VMEM_SPEC,
        scratch_shapes=[pltpu.VMEM((STOPS,) + queries.shape, BF16)]
        + [pltpu.SemaphoreType.DMA((STOPS,))] * 2,
        compiler_params=pltpu.CompilerParams(collective_id=1, has_side_effects=True),
        name="influence",
    )(queries, train)


def local(query_inputs, query_grads, proj_in, proj_out, train_rows, token_owner, token_slot):
    owners = lax.axis_size("blk")
    inputs = (
        token_owner.reshape(1, -1), token_slot.reshape(1, -1),
        proj_out.T, query_grads, proj_in.T, query_inputs, train_rows,
    )
    *inputs, train = [pltpu.with_memory_space_constraint(item, pltpu.HBM) for item in inputs]
    return influence_of(owners, 4 * query_inputs.shape[0] // owners, inputs, train)


def solution(mesh):
    placed = (
        P(("groups", "blk"), None),
        P(("groups", "blk"), None),
        P(),
        P(),
        P(("groups", "blk"), None),
        P(("groups", "blk"), None),
        P(("groups", "blk")),
    )
    return jax.shard_map(
        local,
        mesh=mesh,
        in_specs=placed,
        out_specs=P(None, None, ("groups", "blk")),
        check_vma=False,
    )
```

```python
import functools

import jax
import jax.numpy as jnp
from jax import lax
from jax.experimental import pallas as pl
from jax.experimental.pallas import tpu as pltpu
from jax.sharding import PartitionSpec as P

DOC_DEV = 32
STOPS = 12
NEWTON_STEPS = 6
LEAD = 5
CUT = 2
FLIP = 4
LANES = 128
DOC_GROUP = 8
GROUPS = DOC_DEV // DOC_GROUP
MESH = pl.DeviceIdType.MESH
VMEM_SPEC = pl.BlockSpec(memory_space=pltpu.VMEM)
FAR_SPEC = pl.BlockSpec(memory_space=pl.ANY)
F32 = jnp.float32
BF16 = jnp.bfloat16
CONTRACT_LAST = (((1,), (1,)), ((), ()))


def matmul(left, right):
    return jnp.dot(left, right, preferred_element_type=F32)


def halves(value):
    high = value.astype(BF16)
    return high, (value - high.astype(F32)).astype(BF16)


def pack(owners, capacity, owner_row, slot_row, send_slot, me):
    count = owner_row.shape[1]
    token = lax.broadcasted_iota(jnp.int32, (count, count), 0)
    other = lax.broadcasted_iota(jnp.int32, (count, count), 1)
    earlier = jnp.where(token < other, 1.0, 0.0).astype(BF16)
    owner_id = lax.broadcasted_iota(jnp.int32, (owners, count), 0)
    owner_hot = jnp.where(owner_id == owner_row[...], 1.0, 0.0)
    before = matmul(owner_hot.astype(BF16), earlier)
    rank = jnp.sum(before * owner_hot, axis=0, keepdims=True).astype(jnp.int32)
    position = owner_row[...] * capacity + rank
    place = lax.broadcasted_iota(jnp.int32, (owners * capacity, count), 0)
    placed = jnp.where(place == position, 1.0, 0.0).astype(BF16)
    coded = jnp.where(owner_id == owner_row[...], slot_row[...] + 1, 0).astype(F32).astype(BF16)
    lane = lax.broadcasted_iota(jnp.int32, (LANES, count), 0)
    shift = lax.rem(me, LANES // capacity) * capacity
    spread = jnp.where(lane == rank + shift, 1.0, 0.0).astype(BF16)
    codes = lax.dot_general(coded, spread, CONTRACT_LAST, preferred_element_type=F32)
    codes = codes.astype(jnp.int32)
    for owner in range(owners):
        send_slot[owner] = codes[owner:owner + 1]
    return placed


def greet_all(owners, me):
    barrier = pltpu.get_barrier_semaphore()

    @pl.loop(1, owners)
    def _(ahead):
        pl.semaphore_signal(
            barrier, inc=1, device_id={"blk": lax.rem(me + ahead, owners)}, device_id_type=MESH
        )

    return barrier


def exchange(owners, me, barrier, send_rows, send_slot, recv_rows, recv_slot,
             rows_sent, rows_here, slot_sent, slot_here, during):
    pl.semaphore_wait(barrier, owners - 1)

    def copies(target, source, sem):
        to = {"blk": target}
        return (
            pltpu.make_async_remote_copy(
                src_ref=send_rows.at[target], dst_ref=recv_rows.at[source],
                send_sem=rows_sent.at[target], recv_sem=rows_here.at[sem],
                device_id=to, device_id_type=MESH),
            pltpu.make_async_remote_copy(
                src_ref=send_slot.at[target], dst_ref=recv_slot.at[source],
                send_sem=slot_sent.at[target], recv_sem=slot_here.at[sem],
                device_id=to, device_id_type=MESH),
        )

    @pl.loop(1, owners)
    def _(ahead):
        for copy in copies(lax.rem(me + ahead, owners), me, me):
            copy.start()

    recv_rows[me] = send_rows[me]
    recv_slot[me] = send_slot[me]
    if during is not None:
        during()

    @pl.loop(1, owners)
    def _(ahead):
        source = lax.rem(me + ahead, owners)
        for copy in copies(source, source, source):
            copy.wait_recv()

    def drain():
        @pl.loop(1, owners)
        def _(ahead):
            for copy in copies(lax.rem(me + ahead, owners), me, me):
                copy.wait_send()

    return drain


def gather(owners, capacity, far, near, fetched, low, send_rows, send_slot, recv_rows, recv_slot,
           rows_sent, rows_here, slot_sent, slot_here, during=None):
    me = lax.axis_index("blk")
    fetches = [pltpu.make_async_copy(*pair, fetched.at[i]) for i, pair in enumerate(zip(far, near))]
    for fetch in fetches:
        fetch.start()
    barrier = greet_all(owners, me)
    owner_row, slot_row, p_out, x_grad, p_in, x_in = near
    width = p_in.shape[0]
    for fetch in fetches[:2]:
        fetch.wait()
    placed = pack(owners, capacity, owner_row, slot_row, send_slot, me)
    for at, values, weights, waits in (
        (0, x_grad, p_out, fetches[2:4]), (width, x_in, p_in, fetches[4:6])
    ):
        for fetch in waits:
            fetch.wait()
        low[:, at:at + width] = lax.dot_general(
            values[...], weights[...], CONTRACT_LAST, preferred_element_type=F32
        ).astype(BF16)
    send_rows[...] = matmul(placed, low[...]).astype(BF16).reshape(send_rows.shape)
    return exchange(owners, me, barrier, send_rows, send_slot, recv_rows, recv_slot,
                    rows_sent, rows_here, slot_sent, slot_here, during)


def dispatch_kernel(owners, capacity, *refs):
    far, (recv_rows, recv_slot), near, rest = refs[:6], refs[6:8], refs[8:14], refs[14:]
    drain = gather(owners, capacity, far, near, *rest[:4], recv_rows, recv_slot, *rest[4:])
    drain()


def gather_scratch(owners, capacity, near):
    count, width = near[3].shape[0], near[2].shape[0]
    return [pltpu.VMEM(item.shape, item.dtype) for item in near] + [
        pltpu.SemaphoreType.DMA((len(near),)),
        pltpu.VMEM((count, 2 * width), BF16),
        pltpu.VMEM((owners, capacity, 2 * width), BF16),
        pltpu.VMEM((owners, 1, LANES), jnp.int32),
    ]


def dispatch(owners, capacity, inputs):
    width = inputs[2].shape[0]
    rows = (owners, capacity, 2 * width)
    slots = (owners, 1, LANES)
    return pl.pallas_call(
        functools.partial(dispatch_kernel, owners, capacity),
        out_shape=(jax.ShapeDtypeStruct(rows, BF16), jax.ShapeDtypeStruct(slots, jnp.int32)),
        in_specs=[FAR_SPEC] * len(inputs),
        out_specs=(VMEM_SPEC, VMEM_SPEC),
        scratch_shapes=gather_scratch(owners, capacity, inputs)
        + [pltpu.SemaphoreType.DMA((owners,))] * 4,
        compiler_params=pltpu.CompilerParams(collective_id=0, has_side_effects=True),
        name="dispatch",
    )(*inputs)


def prepare(recv_rows, recv_slot, turned, codes):
    owners, capacity, full = recv_rows.shape
    total = owners * capacity
    group = LANES // capacity
    rows = recv_rows[...].reshape(total, full)
    for part in range(total // LANES):
        span = slice(part * LANES, (part + 1) * LANES)
        turned[:, span] = rows[span].T
        code = recv_slot[part * group]
        for source in range(part * group + 1, (part + 1) * group):
            code = code + recv_slot[source]
        codes[:, span] = code


def beside_each_other(value, left):
    high, low = halves(value)
    right = (1.0 - left.astype(F32)).astype(BF16)
    tops = jnp.concatenate([high * left, low * left], axis=1)
    bottoms = jnp.concatenate([high * right, low * right], axis=1)
    return jnp.concatenate([tops, bottoms, tops, bottoms], axis=0)


def stack(values):
    return jnp.concatenate([jnp.concatenate(halves(value), axis=1) for value in values], axis=0)


def times(lefts, weights):
    product = matmul(stack(lefts), weights)
    lanes = product.shape[1] // 2
    product = product[:, :lanes] + product[:, lanes:]
    rows = lefts[0].shape[0]
    return [product[at * rows:(at + 1) * rows] for at in range(len(lefts))]


def query_group(step, recv_rows, turned, codes, flat, out):
    owners, capacity, full = recv_rows.shape
    width = full // 2
    row = lax.broadcasted_iota(jnp.int32, (width, full), 0)
    col = lax.broadcasted_iota(jnp.int32, (width, full), 1)
    left = lax.broadcasted_iota(jnp.int32, (1, full), 1) < width
    eye = jnp.where((row == col) | (row + width == col), 1.0, 0.0)
    left_half = jnp.where(col < width, 1.0, 0.0).astype(BF16)
    docs = range(DOC_GROUP)
    code = codes[...]
    counts, masked = [], []
    for doc in docs:
        hot = jnp.where(code == step * DOC_GROUP + doc + 1, 1.0, 0.0)
        counts.append(jnp.sum(hot, axis=1, keepdims=True))
        masked.append(turned[...] * hot.astype(BF16))
    rows = recv_rows[...].reshape(owners * capacity, full)
    half = DOC_GROUP // 2
    grams = [
        matmul(jnp.concatenate(masked[at:at + half], axis=0), rows) for at in (0, half)
    ]
    states, sums = [], []
    for doc in docs:
        gram = grams[doc // half][doc % half * full:(doc % half + 1) * full]
        top, bottom = gram[:width], gram[width:]
        damped = jnp.where(left, top, bottom) / (counts[doc] + 1.0) + eye
        spread = jnp.sum(jnp.abs(damped), axis=0, keepdims=True)
        bounds = [
            jnp.max(jnp.where(side, spread, 0.0), axis=1, keepdims=True)
            for side in (left, jnp.logical_not(left))
        ]
        scale = jnp.where(left, 1.0 / bounds[0], 1.0 / bounds[1])
        states.append(eye - damped * scale)
        sums.append(jnp.where(left, eye, top) * scale)
    for level in range(NEWTON_STEPS):
        for doc in docs:
            state, total = states[doc], sums[doc]
            weights = beside_each_other(state, left_half)
            if level < NEWTON_STEPS - 1:
                states[doc], more = times([state, total], weights)
            else:
                more, = times([total], weights)
            sums[doc] = total + more
    zeros = jnp.zeros((width, 2 * full), BF16)
    for doc in docs:
        pieces = stack([sums[doc]])
        flat[doc * width:(doc + 1) * width, :], = times(
            [sums[doc]], jnp.concatenate([pieces, zeros, pieces, zeros], axis=0))
    near = lax.broadcasted_iota(jnp.int32, (DOC_GROUP, full), 1) < width
    for pair in range(width // 2):
        even = flat[pl.ds(2 * pair, DOC_GROUP, stride=width), :]
        odd = flat[pl.ds(2 * pair + 1, DOC_GROUP, stride=width), :]
        both = jnp.where(near, pltpu.roll(even, width, 1), odd)
        out[:, pair * full:(pair + 1) * full] = both.astype(BF16)


def query_scratch(recv_rows):
    owners, capacity, full = recv_rows.shape
    total = owners * capacity
    return [
        pltpu.VMEM((full, total), BF16),
        pltpu.VMEM((1, total), jnp.int32),
        pltpu.VMEM((DOC_GROUP * (full // 2), full), F32),
    ]


def queries_kernel(recv_rows, recv_slot, out, turned, codes, flat):
    prepare(recv_rows, recv_slot, turned, codes)

    @pl.loop(0, GROUPS)
    def _(step):
        query_group(step, recv_rows, turned, codes, flat, out.at[step])


def make_queries(recv_rows, recv_slot):
    width = recv_rows.shape[2] // 2
    return pl.pallas_call(
        queries_kernel,
        out_shape=jax.ShapeDtypeStruct((GROUPS, DOC_GROUP, width * width), BF16),
        in_specs=[VMEM_SPEC] * 2,
        out_specs=VMEM_SPEC,
        scratch_shapes=query_scratch(recv_rows),
        name="queries",
    )(recv_rows, recv_slot).reshape(DOC_DEV, width * width)


def score_into(out, index, block, train):
    out[index] = lax.dot_general(
        block[...], train[...], CONTRACT_LAST, preferred_element_type=F32
    ).astype(BF16)


def window_kernel(owners, queries, train, out, held, sent, here):
    me = lax.axis_index("blk")
    barrier = pltpu.get_barrier_semaphore()

    def peer(stop):
        return lax.rem(me + stop - LEAD + owners, owners)

    def source(stop):
        return lax.rem(me - stop + LEAD + owners, owners)

    def copy(stop):
        return pltpu.make_async_remote_copy(
            src_ref=queries, dst_ref=held.at[stop], send_sem=sent.at[stop],
            recv_sem=here.at[stop], device_id={"blk": peer(stop)}, device_id_type=MESH)

    others = [stop for stop in range(STOPS) if stop != LEAD]
    for stop in others:
        pl.semaphore_signal(
            barrier, inc=1, device_id={"blk": source(stop)}, device_id_type=MESH
        )
    pl.semaphore_wait(barrier, len(others))
    for stop in others:
        copy(stop).start()
    score_into(out, LEAD, queries, train)
    for stop in others:
        copy(stop).wait_recv()
        score_into(out, stop, held.at[stop], train)
    for stop in others:
        copy(stop).wait_send()


def grid_kernel(owners, capacity, *refs):
    far, train_far, out, near = refs[:6], refs[6], refs[7], refs[8:14]
    got, low, send_rows, send_slot, recv_rows, recv_slot = refs[14:20]
    rows_sent, rows_here, slot_sent, slot_here = refs[20:24]
    turned, codes, flat, train, train_turned, fetched, held, sent, here = refs[24:]
    line_size = 4
    me = lax.axis_index("blk")
    core = lax.rem(me, 2)
    side = lax.rem(me // 2, 2)
    line = me // line_size
    to_twin, to_across = 1 - 2 * core, 2 - 4 * side
    twin, across = me + to_twin, me + to_across
    above = lax.rem(me + line_size, owners)
    below = lax.rem(me + owners - line_size, owners)
    beyond = lax.rem(me + 2 * line_size, owners)

    fetch = pltpu.make_async_copy(train_far, train, fetched)

    def flip():
        fetch.start()
        fetch.wait()

        @pl.loop(0, train.shape[1] // (FLIP * LANES))
        def _(step):
            for part in range(FLIP):
                at = pl.multiple_of((step * FLIP + part) * LANES, LANES)
                train_turned[pl.ds(at, LANES), :] = train[:, pl.ds(at, LANES)].T

    drain = gather(owners, capacity, far, near, got, low, send_rows, send_slot, recv_rows, recv_slot,
                   rows_sent, rows_here, slot_sent, slot_here, flip)
    prepare(recv_rows, recv_slot, turned, codes)

    def wrapped(stop):
        return stop % owners if isinstance(stop, int) else lax.rem(stop + 3 * owners, owners)

    def wanted(stop):
        return wrapped(stop) < STOPS

    def when(wish, act):
        if wish is True:
            act()
        else:
            pl.when(wish)(act)

    def skips(some_core):
        return (side == 0) & (some_core == 1) & (line != 1)

    left = side == 0
    own, plus, minus = LEAD, LEAD - line_size, LEAD + line_size
    beside, beside_plus, beside_minus = (LEAD - to_across + turn for turn in (0, -line_size, line_size))
    cross = LEAD - to_across - 2 * line_size
    has_plus = jnp.logical_not(skips(core))
    gives_plus = jnp.logical_not((side == 1) & (core == 1) & (line != 1))
    twin_plus = jnp.logical_not(skips(1 - core))
    has_cross = left | (core == 0)
    twin_cross = left | (core == 1)

    def hands_of(group):
        late = group >= CUT
        turns = ((side == 1) & (core == 0)) | (left & ((line == 0) | (line == 3) | late))
        chains = left & jnp.logical_not(late)
        return (
            (
                (own, None, ((True, above, 0), (True, below, 1), (True, across, 2), (True, twin, 3))),
            ),
            (
                (beside, True, ((turns, beyond, 8), (wanted(beside + to_twin), twin, 9))),
            ),
            (
                (plus, True, ((gives_plus, across, 4), (True, twin, 5))),
                (minus, True, ((True, across, 6), (True, twin, 7))),
            ),
            (
                (beside_plus, has_plus, ((chains & (line == 1), below, 10),
                                         (has_plus & wanted(beside_plus + to_twin), twin, 11))),
                (beside_minus, True, ((chains & (line == 2), above, 12),
                                      (wanted(beside_minus + to_twin), twin, 13))),
            ),
            (
                (cross, has_cross, ((has_cross & wanted(cross + to_twin), twin, 14),)),
            ),
        )

    from_twin = (
        (own, True), (plus, True), (minus, True), (beside, True), (beside_plus, twin_plus),
        (beside_minus, True), (cross, twin_cross),
    )

    def copy(group, mine, sem, device):
        theirs = wrapped(mine + device - me)
        return pltpu.make_async_remote_copy(
            src_ref=held.at[group, wrapped(mine)], dst_ref=held.at[group, theirs],
            send_sem=sent.at[sem, group], recv_sem=here.at[group, theirs],
            device_id={"blk": device}, device_id_type=MESH)

    def arrive(group, mine):
        pltpu.make_async_remote_copy(
            src_ref=held.at[group, wrapped(mine)], dst_ref=held.at[group, wrapped(mine)],
            send_sem=sent.at[0, group], recv_sem=here.at[group, wrapped(mine)],
            device_id={"blk": twin}, device_id_type=MESH).wait_recv()

    def run(group, stage):
        for mine, comes, hands in hands_of(jnp.int32(group))[stage]:
            if comes is not None:
                when(comes, lambda: arrive(group, mine))
            for wish, device, sem in hands:
                when(wish, lambda: copy(group, mine, sem, device).start())

    def sent_by(group):
        for items in hands_of(jnp.int32(group)):
            for mine, _, hands in items:
                for wish, device, sem in hands:
                    when(wish, lambda: copy(group, mine, sem, device).wait_send())

    def run_if(group, stage):
        @pl.when(group >= 0)
        def _():
            run(group, stage)

    def score(group):
        for mine, comes in from_twin:
            slot = mine - to_twin
            wish = wanted(slot) if comes is True else comes & wanted(slot)
            when(wish, lambda: arrive(group, slot))
        block = held[group, :STOPS].reshape(STOPS * DOC_GROUP, train.shape[1])
        tile = matmul(block, train_turned[...])
        out[group] = tile.astype(BF16).reshape(STOPS, DOC_GROUP, train.shape[0])

    @pl.loop(0, GROUPS)
    def _(step):
        query_group(step, recv_rows, turned, codes, flat, held.at[step, own])
        run(step, 0)
        run_if(step - 2, 2)
        run_if(step - 2, 1)

    drain()
    run(2, 1)
    run(2, 2)
    run(0, 3)
    run(0, 4)
    run(3, 1)
    run(1, 3)
    score(0)
    run(3, 2)
    run(1, 4)
    score(1)
    run(2, 3)
    run(2, 4)
    run(3, 3)
    score(2)
    run(3, 4)
    score(3)
    pl.loop(0, GROUPS)(sent_by)


def influence_of(owners, capacity, inputs, train):
    width = inputs[2].shape[0]
    if owners == 16:
        recv_rows = jax.ShapeDtypeStruct((owners, capacity, 2 * width), BF16)
        tiles = pl.pallas_call(
            functools.partial(grid_kernel, owners, capacity),
            out_shape=jax.ShapeDtypeStruct((GROUPS, STOPS, DOC_GROUP, train.shape[0]), BF16),
            in_specs=[FAR_SPEC] * (len(inputs) + 1),
            out_specs=VMEM_SPEC,
            scratch_shapes=gather_scratch(owners, capacity, inputs)
            + [pltpu.VMEM(recv_rows.shape, BF16), pltpu.VMEM((owners, 1, LANES), jnp.int32)]
            + [pltpu.SemaphoreType.DMA((owners,))] * 4
            + query_scratch(recv_rows)
            + [pltpu.VMEM(train.shape, BF16), pltpu.VMEM(train.shape[::-1], BF16)]
            + [pltpu.SemaphoreType.DMA]
            + [pltpu.VMEM((GROUPS, owners, DOC_GROUP, train.shape[1]), BF16)]
            + [pltpu.SemaphoreType.DMA((15, GROUPS)), pltpu.SemaphoreType.DMA((GROUPS, owners))],
            compiler_params=pltpu.CompilerParams(
                collective_id=0, has_side_effects=True, vmem_limit_bytes=32 << 20),
            name="influence",
        )(*inputs, train)
        return tiles.transpose(1, 0, 2, 3).reshape(STOPS, DOC_DEV, train.shape[0])
    queries = make_queries(*dispatch(owners, capacity, inputs))
    return pl.pallas_call(
        functools.partial(window_kernel, owners),
        out_shape=jax.ShapeDtypeStruct((STOPS, DOC_DEV, train.shape[0]), BF16),
        in_specs=[VMEM_SPEC] * 2,
        out_specs=VMEM_SPEC,
        scratch_shapes=[pltpu.VMEM((STOPS,) + queries.shape, BF16)]
        + [pltpu.SemaphoreType.DMA((STOPS,))] * 2,
        compiler_params=pltpu.CompilerParams(collective_id=1, has_side_effects=True),
        name="influence",
    )(queries, train)


def local(query_inputs, query_grads, proj_in, proj_out, train_rows, token_owner, token_slot):
    owners = lax.axis_size("blk")
    inputs = (
        token_owner.reshape(1, -1), token_slot.reshape(1, -1),
        proj_out.T, query_grads, proj_in.T, query_inputs, train_rows,
    )
    *inputs, train = [pltpu.with_memory_space_constraint(item, pltpu.HBM) for item in inputs]
    return influence_of(owners, 4 * query_inputs.shape[0] // owners, inputs, train)


def solution(mesh):
    placed = (
        P(("groups", "blk"), None),
        P(("groups", "blk"), None),
        P(),
        P(),
        P(("groups", "blk"), None),
        P(("groups", "blk"), None),
        P(("groups", "blk")),
    )
    return jax.shard_map(
        local,
        mesh=mesh,
        in_specs=placed,
        out_specs=P(None, None, ("groups", "blk")),
        check_vma=False,
    )
```

```python
import functools

import jax
import jax.numpy as jnp
from jax import lax
from jax.experimental import pallas as pl
from jax.experimental.pallas import tpu as pltpu
from jax.sharding import PartitionSpec as P

DOC_DEV = 32
STOPS = 12
NEWTON_STEPS = 6
LEAD = 5
CUT = 2
FLIP = 4
LANES = 128
DOC_GROUP = 8
GROUPS = DOC_DEV // DOC_GROUP
MESH = pl.DeviceIdType.MESH
VMEM_SPEC = pl.BlockSpec(memory_space=pltpu.VMEM)
FAR_SPEC = pl.BlockSpec(memory_space=pl.ANY)
F32 = jnp.float32
BF16 = jnp.bfloat16
CONTRACT_LAST = (((1,), (1,)), ((), ()))


def matmul(left, right):
    return jnp.dot(left, right, preferred_element_type=F32)


def halves(value):
    high = value.astype(BF16)
    return high, (value - high.astype(F32)).astype(BF16)


def pack(owners, capacity, owner_row, slot_row, send_slot, me):
    count = owner_row.shape[1]
    token = lax.broadcasted_iota(jnp.int32, (count, count), 0)
    other = lax.broadcasted_iota(jnp.int32, (count, count), 1)
    earlier = jnp.where(token < other, 1.0, 0.0).astype(BF16)
    owner_id = lax.broadcasted_iota(jnp.int32, (owners, count), 0)
    owner_hot = jnp.where(owner_id == owner_row[...], 1.0, 0.0)
    before = matmul(owner_hot.astype(BF16), earlier)
    rank = jnp.sum(before * owner_hot, axis=0, keepdims=True).astype(jnp.int32)
    position = owner_row[...] * capacity + rank
    place = lax.broadcasted_iota(jnp.int32, (owners * capacity, count), 0)
    placed = jnp.where(place == position, 1.0, 0.0).astype(BF16)
    coded = jnp.where(owner_id == owner_row[...], slot_row[...] + 1, 0).astype(F32).astype(BF16)
    lane = lax.broadcasted_iota(jnp.int32, (LANES, count), 0)
    shift = lax.rem(me, LANES // capacity) * capacity
    spread = jnp.where(lane == rank + shift, 1.0, 0.0).astype(BF16)
    codes = lax.dot_general(coded, spread, CONTRACT_LAST, preferred_element_type=F32)
    codes = codes.astype(jnp.int32)
    for owner in range(owners):
        send_slot[owner] = codes[owner:owner + 1]
    return placed


def greet_all(owners, me):
    barrier = pltpu.get_barrier_semaphore()

    @pl.loop(1, owners)
    def _(ahead):
        pl.semaphore_signal(
            barrier, inc=1, device_id={"blk": lax.rem(me + ahead, owners)}, device_id_type=MESH
        )

    return barrier


def exchange(owners, me, barrier, send_rows, send_slot, recv_rows, recv_slot,
             rows_sent, rows_here, slot_sent, slot_here, during):
    pl.semaphore_wait(barrier, owners - 1)

    def copies(target, source, sem):
        to = {"blk": target}
        return (
            pltpu.make_async_remote_copy(
                src_ref=send_rows.at[target], dst_ref=recv_rows.at[source],
                send_sem=rows_sent.at[target], recv_sem=rows_here.at[sem],
                device_id=to, device_id_type=MESH),
            pltpu.make_async_remote_copy(
                src_ref=send_slot.at[target], dst_ref=recv_slot.at[source],
                send_sem=slot_sent.at[target], recv_sem=slot_here.at[sem],
                device_id=to, device_id_type=MESH),
        )

    @pl.loop(1, owners)
    def _(ahead):
        for copy in copies(lax.rem(me + ahead, owners), me, me):
            copy.start()

    recv_rows[me] = send_rows[me]
    recv_slot[me] = send_slot[me]
    if during is not None:
        during()

    @pl.loop(1, owners)
    def _(ahead):
        source = lax.rem(me + ahead, owners)
        for copy in copies(source, source, source):
            copy.wait_recv()

    def drain():
        @pl.loop(1, owners)
        def _(ahead):
            for copy in copies(lax.rem(me + ahead, owners), me, me):
                copy.wait_send()

    return drain


def gather(owners, capacity, far, near, fetched, low, send_rows, send_slot, recv_rows, recv_slot,
           rows_sent, rows_here, slot_sent, slot_here, during=None):
    me = lax.axis_index("blk")
    fetches = [pltpu.make_async_copy(*pair, fetched.at[i]) for i, pair in enumerate(zip(far, near))]
    for fetch in fetches:
        fetch.start()
    barrier = greet_all(owners, me)
    owner_row, slot_row, p_out, x_grad, p_in, x_in = near
    width = p_in.shape[0]
    for fetch in fetches[:2]:
        fetch.wait()
    placed = pack(owners, capacity, owner_row, slot_row, send_slot, me)
    for at, values, weights, waits in (
        (0, x_grad, p_out, fetches[2:4]), (width, x_in, p_in, fetches[4:6])
    ):
        for fetch in waits:
            fetch.wait()
        low[:, at:at + width] = lax.dot_general(
            values[...], weights[...], CONTRACT_LAST, preferred_element_type=F32
        ).astype(BF16)
    send_rows[...] = matmul(placed, low[...]).astype(BF16).reshape(send_rows.shape)
    return exchange(owners, me, barrier, send_rows, send_slot, recv_rows, recv_slot,
                    rows_sent, rows_here, slot_sent, slot_here, during)


def dispatch_kernel(owners, capacity, *refs):
    far, (recv_rows, recv_slot), near, rest = refs[:6], refs[6:8], refs[8:14], refs[14:]
    drain = gather(owners, capacity, far, near, *rest[:4], recv_rows, recv_slot, *rest[4:])
    drain()


def gather_scratch(owners, capacity, near):
    count, width = near[3].shape[0], near[2].shape[0]
    return [pltpu.VMEM(item.shape, item.dtype) for item in near] + [
        pltpu.SemaphoreType.DMA((len(near),)),
        pltpu.VMEM((count, 2 * width), BF16),
        pltpu.VMEM((owners, capacity, 2 * width), BF16),
        pltpu.VMEM((owners, 1, LANES), jnp.int32),
    ]


def dispatch(owners, capacity, inputs):
    width = inputs[2].shape[0]
    rows = (owners, capacity, 2 * width)
    slots = (owners, 1, LANES)
    return pl.pallas_call(
        functools.partial(dispatch_kernel, owners, capacity),
        out_shape=(jax.ShapeDtypeStruct(rows, BF16), jax.ShapeDtypeStruct(slots, jnp.int32)),
        in_specs=[FAR_SPEC] * len(inputs),
        out_specs=(VMEM_SPEC, VMEM_SPEC),
        scratch_shapes=gather_scratch(owners, capacity, inputs)
        + [pltpu.SemaphoreType.DMA((owners,))] * 4,
        compiler_params=pltpu.CompilerParams(collective_id=0, has_side_effects=True),
        name="dispatch",
    )(*inputs)


def prepare(recv_rows, recv_slot, turned, codes):
    owners, capacity, full = recv_rows.shape
    total = owners * capacity
    group = LANES // capacity
    rows = recv_rows[...].reshape(total, full)
    for part in range(total // LANES):
        span = slice(part * LANES, (part + 1) * LANES)
        turned[:, span] = rows[span].T
        code = recv_slot[part * group]
        for source in range(part * group + 1, (part + 1) * group):
            code = code + recv_slot[source]
        codes[:, span] = code


def beside_each_other(value, left):
    high, low = halves(value)
    tops = jnp.concatenate([high * left, low * left], axis=1)
    bottoms = jnp.concatenate([high, low], axis=1) - tops
    return jnp.concatenate([tops, bottoms, tops, bottoms], axis=0)


def stack(values):
    return jnp.concatenate([jnp.concatenate(halves(value), axis=1) for value in values], axis=0)


def times(lefts, weights):
    product = matmul(stack(lefts), weights)
    lanes = product.shape[1] // 2
    product = product[:, :lanes] + product[:, lanes:]
    rows = lefts[0].shape[0]
    return [product[at * rows:(at + 1) * rows] for at in range(len(lefts))]


def query_group(step, recv_rows, turned, codes, flat, out):
    owners, capacity, full = recv_rows.shape
    width = full // 2
    row = lax.broadcasted_iota(jnp.int32, (width, full), 0)
    col = lax.broadcasted_iota(jnp.int32, (width, full), 1)
    left = lax.broadcasted_iota(jnp.int32, (1, full), 1) < width
    eye = jnp.where((row == col) | (row + width == col), 1.0, 0.0)
    left_half = jnp.where(col < width, 1.0, 0.0).astype(BF16)
    docs = range(DOC_GROUP)
    code = codes[...]
    counts, masked = [], []
    for doc in docs:
        hot = jnp.where(code == step * DOC_GROUP + doc + 1, 1.0, 0.0)
        counts.append(jnp.sum(hot, axis=1, keepdims=True))
        masked.append(turned[...] * hot.astype(BF16))
    rows = recv_rows[...].reshape(owners * capacity, full)
    half = DOC_GROUP // 2
    grams = [
        matmul(jnp.concatenate(masked[at:at + half], axis=0), rows) for at in (0, half)
    ]
    states, sums = [], []
    for doc in docs:
        gram = grams[doc // half][doc % half * full:(doc % half + 1) * full]
        top, bottom = gram[:width], gram[width:]
        damped = jnp.where(left, top, bottom) * (1.0 / (counts[doc] + 1.0)) + eye
        spread = jnp.sum(jnp.abs(damped), axis=0, keepdims=True)
        bounds = [
            jnp.max(jnp.where(side, spread, 0.0), axis=1, keepdims=True)
            for side in (left, jnp.logical_not(left))
        ]
        scale = jnp.where(left, 1.0 / bounds[0], 1.0 / bounds[1])
        states.append(eye - damped * scale)
        sums.append(jnp.where(left, eye, top) * scale)
    for level in range(NEWTON_STEPS):
        for doc in docs:
            state, total = states[doc], sums[doc]
            weights = beside_each_other(state, left_half)
            if level < NEWTON_STEPS - 1:
                states[doc], more = times([state, total], weights)
            else:
                more, = times([total], weights)
            sums[doc] = total + more
    zeros = jnp.zeros((width, 2 * full), BF16)
    for doc in docs:
        pieces = stack([sums[doc]])
        flat[doc * width:(doc + 1) * width, :], = times(
            [sums[doc]], jnp.concatenate([pieces, zeros, pieces, zeros], axis=0))
    near = lax.broadcasted_iota(jnp.int32, (DOC_GROUP, full), 1) < width
    for pair in range(width // 2):
        even = flat[pl.ds(2 * pair, DOC_GROUP, stride=width), :]
        odd = flat[pl.ds(2 * pair + 1, DOC_GROUP, stride=width), :]
        both = jnp.where(near, pltpu.roll(even, width, 1), odd)
        out[:, pair * full:(pair + 1) * full] = both.astype(BF16)


def query_scratch(recv_rows):
    owners, capacity, full = recv_rows.shape
    total = owners * capacity
    return [
        pltpu.VMEM((full, total), BF16),
        pltpu.VMEM((1, total), jnp.int32),
        pltpu.VMEM((DOC_GROUP * (full // 2), full), F32),
    ]


def queries_kernel(recv_rows, recv_slot, out, turned, codes, flat):
    prepare(recv_rows, recv_slot, turned, codes)

    @pl.loop(0, GROUPS)
    def _(step):
        query_group(step, recv_rows, turned, codes, flat, out.at[step])


def make_queries(recv_rows, recv_slot):
    width = recv_rows.shape[2] // 2
    return pl.pallas_call(
        queries_kernel,
        out_shape=jax.ShapeDtypeStruct((GROUPS, DOC_GROUP, width * width), BF16),
        in_specs=[VMEM_SPEC] * 2,
        out_specs=VMEM_SPEC,
        scratch_shapes=query_scratch(recv_rows),
        name="queries",
    )(recv_rows, recv_slot).reshape(DOC_DEV, width * width)


def score_into(out, index, block, train):
    out[index] = lax.dot_general(
        block[...], train[...], CONTRACT_LAST, preferred_element_type=F32
    ).astype(BF16)


def window_kernel(owners, queries, train, out, held, sent, here):
    me = lax.axis_index("blk")
    barrier = pltpu.get_barrier_semaphore()

    def peer(stop):
        return lax.rem(me + stop - LEAD + owners, owners)

    def source(stop):
        return lax.rem(me - stop + LEAD + owners, owners)

    def copy(stop):
        return pltpu.make_async_remote_copy(
            src_ref=queries, dst_ref=held.at[stop], send_sem=sent.at[stop],
            recv_sem=here.at[stop], device_id={"blk": peer(stop)}, device_id_type=MESH)

    others = [stop for stop in range(STOPS) if stop != LEAD]
    for stop in others:
        pl.semaphore_signal(
            barrier, inc=1, device_id={"blk": source(stop)}, device_id_type=MESH
        )
    pl.semaphore_wait(barrier, len(others))
    for stop in others:
        copy(stop).start()
    score_into(out, LEAD, queries, train)
    for stop in others:
        copy(stop).wait_recv()
        score_into(out, stop, held.at[stop], train)
    for stop in others:
        copy(stop).wait_send()


def grid_kernel(owners, capacity, *refs):
    far, train_far, out, near = refs[:6], refs[6], refs[7], refs[8:14]
    got, low, send_rows, send_slot, recv_rows, recv_slot = refs[14:20]
    rows_sent, rows_here, slot_sent, slot_here = refs[20:24]
    turned, codes, flat, train, train_turned, fetched, held, sent, here = refs[24:]
    line_size = 4
    me = lax.axis_index("blk")
    core = lax.rem(me, 2)
    side = lax.rem(me // 2, 2)
    line = me // line_size
    to_twin, to_across = 1 - 2 * core, 2 - 4 * side
    twin, across = me + to_twin, me + to_across
    above = lax.rem(me + line_size, owners)
    below = lax.rem(me + owners - line_size, owners)
    beyond = lax.rem(me + 2 * line_size, owners)

    fetch = pltpu.make_async_copy(train_far, train, fetched)

    def flip():
        fetch.start()
        fetch.wait()

        @pl.loop(0, train.shape[1] // (FLIP * LANES))
        def _(step):
            for part in range(FLIP):
                at = pl.multiple_of((step * FLIP + part) * LANES, LANES)
                train_turned[pl.ds(at, LANES), :] = train[:, pl.ds(at, LANES)].T

    drain = gather(owners, capacity, far, near, got, low, send_rows, send_slot, recv_rows, recv_slot,
                   rows_sent, rows_here, slot_sent, slot_here, flip)
    prepare(recv_rows, recv_slot, turned, codes)

    def wrapped(stop):
        return stop % owners if isinstance(stop, int) else lax.rem(stop + 3 * owners, owners)

    def wanted(stop):
        return wrapped(stop) < STOPS

    def when(wish, act):
        if wish is True:
            act()
        else:
            pl.when(wish)(act)

    def skips(some_core):
        return (side == 0) & (some_core == 1) & (line != 1)

    left = side == 0
    own, plus, minus = LEAD, LEAD - line_size, LEAD + line_size
    beside, beside_plus, beside_minus = (LEAD - to_across + turn for turn in (0, -line_size, line_size))
    cross = LEAD - to_across - 2 * line_size
    has_plus = jnp.logical_not(skips(core))
    gives_plus = jnp.logical_not((side == 1) & (core == 1) & (line != 1))
    twin_plus = jnp.logical_not(skips(1 - core))
    has_cross = left | (core == 0)
    twin_cross = left | (core == 1)

    def hands_of(group):
        late = group >= CUT
        turns = ((side == 1) & (core == 0)) | (left & ((line == 0) | (line == 3) | late))
        chains = left & jnp.logical_not(late)
        return (
            (
                (own, None, ((True, across, 2), (True, above, 0), (True, below, 1), (True, twin, 3))),
            ),
            (
                (beside, True, ((turns, beyond, 8), (wanted(beside + to_twin), twin, 9))),
            ),
            (
                (plus, True, ((gives_plus, across, 4), (True, twin, 5))),
                (minus, True, ((True, across, 6), (True, twin, 7))),
            ),
            (
                (beside_plus, has_plus, ((chains & (line == 1), below, 10),
                                         (has_plus & wanted(beside_plus + to_twin), twin, 11))),
                (beside_minus, True, ((chains & (line == 2), above, 12),
                                      (wanted(beside_minus + to_twin), twin, 13))),
            ),
            (
                (cross, has_cross, ((has_cross & wanted(cross + to_twin), twin, 14),)),
            ),
        )

    from_twin = (
        (own, True), (plus, True), (minus, True), (beside, True), (beside_plus, twin_plus),
        (beside_minus, True), (cross, twin_cross),
    )

    def copy(group, mine, sem, device):
        theirs = wrapped(mine + device - me)
        return pltpu.make_async_remote_copy(
            src_ref=held.at[group, wrapped(mine)], dst_ref=held.at[group, theirs],
            send_sem=sent.at[sem, group], recv_sem=here.at[group, theirs],
            device_id={"blk": device}, device_id_type=MESH)

    def arrive(group, mine):
        pltpu.make_async_remote_copy(
            src_ref=held.at[group, wrapped(mine)], dst_ref=held.at[group, wrapped(mine)],
            send_sem=sent.at[0, group], recv_sem=here.at[group, wrapped(mine)],
            device_id={"blk": twin}, device_id_type=MESH).wait_recv()

    def run(group, stage):
        for mine, comes, hands in hands_of(jnp.int32(group))[stage]:
            if comes is not None:
                when(comes, lambda: arrive(group, mine))
            for wish, device, sem in hands:
                when(wish, lambda: copy(group, mine, sem, device).start())

    def sent_by(group):
        for items in hands_of(jnp.int32(group)):
            for mine, _, hands in items:
                for wish, device, sem in hands:
                    when(wish, lambda: copy(group, mine, sem, device).wait_send())

    def run_if(group, stage):
        @pl.when(group >= 0)
        def _():
            run(group, stage)

    def score(group):
        for mine, comes in from_twin:
            slot = mine - to_twin
            wish = wanted(slot) if comes is True else comes & wanted(slot)
            when(wish, lambda: arrive(group, slot))
        block = held[group, :STOPS].reshape(STOPS * DOC_GROUP, train.shape[1])
        tile = matmul(block, train_turned[...])
        out[group] = tile.astype(BF16).reshape(STOPS, DOC_GROUP, train.shape[0])

    @pl.loop(0, GROUPS)
    def _(step):
        query_group(step, recv_rows, turned, codes, flat, held.at[step, own])
        run(step, 0)
        run_if(step - 2, 2)
        run_if(step - 2, 1)

    drain()
    run(2, 2)
    run(2, 1)
    run(0, 3)
    run(3, 1)
    run(0, 4)
    score(0)
    run(1, 3)
    run(3, 2)
    run(1, 4)
    run(2, 3)
    score(1)
    run(2, 4)
    run(3, 3)
    score(2)
    run(3, 4)
    score(3)
    pl.loop(0, GROUPS)(sent_by)


def influence_of(owners, capacity, inputs, train):
    width = inputs[2].shape[0]
    if owners == 16:
        recv_rows = jax.ShapeDtypeStruct((owners, capacity, 2 * width), BF16)
        tiles = pl.pallas_call(
            functools.partial(grid_kernel, owners, capacity),
            out_shape=jax.ShapeDtypeStruct((GROUPS, STOPS, DOC_GROUP, train.shape[0]), BF16),
            in_specs=[FAR_SPEC] * (len(inputs) + 1),
            out_specs=VMEM_SPEC,
            scratch_shapes=gather_scratch(owners, capacity, inputs)
            + [pltpu.VMEM(recv_rows.shape, BF16), pltpu.VMEM((owners, 1, LANES), jnp.int32)]
            + [pltpu.SemaphoreType.DMA((owners,))] * 4
            + query_scratch(recv_rows)
            + [pltpu.VMEM(train.shape, BF16), pltpu.VMEM(train.shape[::-1], BF16)]
            + [pltpu.SemaphoreType.DMA]
            + [pltpu.VMEM((GROUPS, owners, DOC_GROUP, train.shape[1]), BF16)]
            + [pltpu.SemaphoreType.DMA((15, GROUPS)), pltpu.SemaphoreType.DMA((GROUPS, owners))],
            compiler_params=pltpu.CompilerParams(
                collective_id=0, has_side_effects=True, vmem_limit_bytes=32 << 20),
            name="influence",
        )(*inputs, train)
        return tiles.transpose(1, 0, 2, 3).reshape(STOPS, DOC_DEV, train.shape[0])
    queries = make_queries(*dispatch(owners, capacity, inputs))
    return pl.pallas_call(
        functools.partial(window_kernel, owners),
        out_shape=jax.ShapeDtypeStruct((STOPS, DOC_DEV, train.shape[0]), BF16),
        in_specs=[VMEM_SPEC] * 2,
        out_specs=VMEM_SPEC,
        scratch_shapes=[pltpu.VMEM((STOPS,) + queries.shape, BF16)]
        + [pltpu.SemaphoreType.DMA((STOPS,))] * 2,
        compiler_params=pltpu.CompilerParams(collective_id=1, has_side_effects=True),
        name="influence",
    )(queries, train)


def local(query_inputs, query_grads, proj_in, proj_out, train_rows, token_owner, token_slot):
    owners = lax.axis_size("blk")
    inputs = (
        token_owner.reshape(1, -1), token_slot.reshape(1, -1),
        proj_out.T, query_grads, proj_in.T, query_inputs, train_rows,
    )
    *inputs, train = [pltpu.with_memory_space_constraint(item, pltpu.HBM) for item in inputs]
    return influence_of(owners, 4 * query_inputs.shape[0] // owners, inputs, train)


def solution(mesh):
    placed = (
        P(("groups", "blk"), None),
        P(("groups", "blk"), None),
        P(),
        P(),
        P(("groups", "blk"), None),
        P(("groups", "blk"), None),
        P(("groups", "blk")),
    )
    return jax.shard_map(
        local,
        mesh=mesh,
        in_specs=placed,
        out_specs=P(None, None, ("groups", "blk")),
        check_vma=False,
    )
```
